256 devices in a mesh: gx: 32 (over z, x), gy: 4 (over y_lo, core), gz: 2 (over y_hi).
Axes of the slice: x: 4, y: 4 (y_hi: 2, y_lo: 2; y = y_hi * 2 + y_lo), z: 8, core: 2. Of those that a mesh axis runs over, the one named last changes fastest.
Arguments:
- coarse_fields: float32 [4, 512, 64, 256], P(None, 'gx', 'gy', 'gz'), may hold values from -6 to 6
- coarse_wind: float32 [3, 512, 64, 256], P(None, 'gx', 'gy', 'gz'), may hold values from -0.4 to 0.4
- fine_fields: float32 [4, 1024, 64, 256], P(None, 'gx', 'gy', 'gz'), may hold values from -6 to 6
- fine_wind: float32 [3, 1024, 64, 256], P(None, 'gx', 'gy', 'gz'), may hold values from -0.4 to 0.4
- fine_owner: int32 [32, 4, 2], P('gx', 'gy', 'gz'), may hold values from 0 to 31, as said below
Outputs:
- coarse_next: float32 [4, 512, 64, 256], P(None, 'gx', 'gy', 'gz')
- fine_next: float32 [4, 1024, 64, 256], P(None, 'gx', 'gy', 'gz')
The draws below stay inside these ranges and needn't reach their ends.
Inputs may be any that keep to these rules, and one draw needn't show every extreme that they name: `fine_owner`: in each row of fine boxes along the first direction (fixed second and third index), fine box i refines coarse box (i + r) mod 32 for an offset r of that row, so every row names every coarse box once.
All inputs are finite; a program needn't handle non-finite values.
Results may differ from the reference program's by a relative error of at most 0.0003.
Values sent between devices are 32-bit elements; how exact they have to be, the bound alone decides.
A program may use at most 128 MiB of HBM per device.

```python
import jax
import jax.numpy as jnp
from jax import lax

FIELDS = 4
RATIO = 2
BOX_X = 16
BOX_Y = 16
BOX_Z = 128
BOXES_X = 32
BOXES_Y = 4
BOXES_Z = 2
NX = 512
NY = 64
NZ = 256
FINE_X = 1024
FINE_Y = 64
FINE_Z = 256


def draw_fine_owner(key, part):
    row_count = BOXES_Y * BOXES_Z
    key_extra = jax.random.fold_in(key, 11)
    key_order = jax.random.fold_in(key, 23)
    extra = jax.random.randint(key_extra, (row_count,), 0, BOXES_X)
    places = jnp.arange(row_count)
    planted = jnp.where(places == 0, BOXES_X - 1, jnp.where(places == 1, BOXES_X // 2, jnp.where(places == 2, 1 % BOXES_X, extra)))
    order = jax.random.permutation(key_order, row_count)
    row_offset = planted[order].reshape(BOXES_Y, BOXES_Z)
    box_index = jnp.arange(BOXES_X)[:, None, None]
    return ((box_index + row_offset[None]) % BOXES_X).astype(jnp.int32)


def block_levels(stream_key, shape, pieces, least, high):
    loudness = 1.0
    for axis_at, shards_of in pieces:
        heights = jax.random.uniform(jax.random.fold_in(jax.random.fold_in(stream_key, 6), axis_at), (shards_of,), jnp.float32, least / len(pieces), high / len(pieces))
        loudness = loudness * jnp.repeat(jnp.exp(heights), shape[axis_at] // shards_of).reshape((-1,) + (1,) * (len(shape) - 1 - axis_at))
    return loudness


def normal_values(key, shape, deviation, bound, shards=(), held_as=jnp.bfloat16):
    entries = deviation * jax.random.normal(key, shape, jnp.float32)
    if shards:
        entries = entries * block_levels(key, shape, shards, -0.22, 0.18)
    return jnp.clip(entries, -bound, bound).astype(held_as)


def setup_inputs(seed: int = 0) -> dict:
    seeds = jax.random.split(jax.random.key(seed), 6)
    return {
        "coarse_fields": normal_values(seeds[0], (FIELDS, NX, NY, NZ), 1.0, 6.0, ((1, 32), (2, 4), (3, 2)), jnp.float32),
        "coarse_wind": jnp.clip(jax.random.uniform(seeds[1], (3, NX, NY, NZ), jnp.float32, -0.4, 0.4) * block_levels(seeds[1], (3, NX, NY, NZ), ((1, 32), (2, 4), (3, 2)), -0.4, 0.0), -0.4, 0.4),
        "fine_fields": normal_values(seeds[2], (FIELDS, FINE_X, FINE_Y, FINE_Z), 1.0, 6.0, ((1, 32), (2, 4), (3, 2)), jnp.float32),
        "fine_wind": jnp.clip(jax.random.uniform(seeds[3], (3, FINE_X, FINE_Y, FINE_Z), jnp.float32, -0.4, 0.4) * block_levels(seeds[3], (3, FINE_X, FINE_Y, FINE_Z), ((1, 32), (2, 4), (3, 2)), -0.4, 0.0), -0.4, 0.4),
        "fine_owner": draw_fine_owner(jax.random.fold_in(seeds[5], 71), 0),
    }


diffusion = 0.05
section_weights = (1.0 / 3.0, 0.5, 1.0)


def tendency(padded, velocity):
    center = padded[:, 1:-1, 1:-1, 1:-1]
    along_first = padded[:, 2:, 1:-1, 1:-1] - padded[:, :-2, 1:-1, 1:-1]
    along_second = padded[:, 1:-1, 2:, 1:-1] - padded[:, 1:-1, :-2, 1:-1]
    along_third = padded[:, 1:-1, 1:-1, 2:] - padded[:, 1:-1, 1:-1, :-2]
    beside_all = (padded[:, 2:, 1:-1, 1:-1] + padded[:, :-2, 1:-1, 1:-1]) + (padded[:, 1:-1, 2:, 1:-1] + padded[:, 1:-1, :-2, 1:-1]) + (padded[:, 1:-1, 1:-1, 2:] + padded[:, 1:-1, 1:-1, :-2])
    advect = velocity[0] * along_first + velocity[1] * along_second + velocity[2] * along_third
    return -0.5 * advect + diffusion * (beside_all - 6.0 * center)


def refine(coarse, direction):
    length = coarse.shape[direction]
    low_part = lax.slice_in_dim(coarse, 0, length - 1, axis=direction)
    high_part = lax.slice_in_dim(coarse, 1, length, axis=direction)
    odd_cells = 0.75 * low_part + 0.25 * high_part
    even_cells = 0.25 * low_part + 0.75 * high_part
    paired = jnp.stack((odd_cells, even_cells), axis=direction + 1)
    target = list(coarse.shape)
    target[direction] = 2 * (length - 1)
    return paired.reshape(target)


def coarse_slabs(padded, lead_y, span_y, lead_z, span_z):
    rows_y = jnp.concatenate((padded[:, :, lead_y:lead_y + 2], padded[:, :, lead_y + span_y:lead_y + span_y + 2]), axis=2)
    slab_y = rows_y[:, :, :, lead_z:lead_z + span_z + 2]
    rows_z = jnp.concatenate((padded[:, :, :, lead_z:lead_z + 2], padded[:, :, :, lead_z + span_z:lead_z + span_z + 2]), axis=3)
    slab_z = rows_z[:, :, lead_y:lead_y + span_y + 2, :]
    return slab_y, slab_z


def slab_faces(slab_y, slab_z):
    wide_y = refine(slab_y, 1)[:, 1:-1]
    low_y = 0.75 * wide_y[:, :, 0] + 0.25 * wide_y[:, :, 1]
    high_y = 0.25 * wide_y[:, :, 2] + 0.75 * wide_y[:, :, 3]
    faces_y = refine(jnp.stack((low_y, high_y), axis=2), 3)[:, :, :, 1:-1]
    wide_z = refine(refine(slab_z, 1)[:, 1:-1], 2)[:, :, 1:-1]
    low_z = 0.75 * wide_z[:, :, :, 0] + 0.25 * wide_z[:, :, :, 1]
    high_z = 0.25 * wide_z[:, :, :, 2] + 0.75 * wide_z[:, :, :, 3]
    faces_z = jnp.stack((low_z, high_z), axis=3)
    return faces_y, faces_z


def fine_padded(widened, faces_y, faces_z):
    padded = jnp.pad(widened, ((0, 0), (0, 0), (1, 1), (1, 1)))
    padded = padded.at[:, 1:-1, 0, 1:-1].set(faces_y[:, :, 0])
    padded = padded.at[:, 1:-1, -1, 1:-1].set(faces_y[:, :, 1])
    padded = padded.at[:, 1:-1, 1:-1, 0].set(faces_z[:, :, :, 0])
    padded = padded.at[:, 1:-1, 1:-1, -1].set(faces_z[:, :, :, 1])
    return padded


def coarsen(fine):
    blocks = fine.reshape(fine.shape[0], fine.shape[1] // 2, 2, fine.shape[2] // 2, 2, fine.shape[3] // 2, 2)
    return 0.125 * jnp.sum(blocks, axis=(2, 4, 6))


def split_boxes(whole, size_x, size_y, size_z):
    shaped = whole.reshape(whole.shape[0], whole.shape[1] // size_x, size_x, whole.shape[2] // size_y, size_y, whole.shape[3] // size_z, size_z)
    return shaped.transpose(1, 3, 5, 0, 2, 4, 6)


def join_boxes(boxes):
    shaped = boxes.transpose(3, 0, 4, 1, 5, 2, 6)
    return shaped.reshape(boxes.shape[3], boxes.shape[0] * boxes.shape[4], boxes.shape[1] * boxes.shape[5], boxes.shape[2] * boxes.shape[6])


def reference(coarse_fields, coarse_wind, fine_fields, fine_wind, fine_owner):
    lead_y = BOX_Y // 4
    span_y = BOX_Y // 2
    lead_z = BOX_Z // 4
    span_z = BOX_Z // 2
    total_boxes = BOXES_X * BOXES_Y * BOXES_Z
    rows_y = jnp.arange(BOXES_Y)[None, :, None]
    rows_z = jnp.arange(BOXES_Z)[None, None, :]
    fine_x = RATIO * BOX_X
    wind_boxes = split_boxes(fine_wind, fine_x, BOX_Y, BOX_Z).reshape((total_boxes, 3, fine_x, BOX_Y, BOX_Z))
    coarse_state = coarse_fields
    fine_state = fine_fields
    for fraction in section_weights:
        wrapped = jnp.pad(coarse_state, ((0, 0), (1, 1), (1, 1), (0, 0)), mode="wrap")
        padded = jnp.pad(wrapped, ((0, 0), (0, 0), (0, 0), (1, 1)))
        coarse_rate = tendency(padded, coarse_wind)

        def box_faces(number):
            index_x = (number // (BOXES_Y * BOXES_Z)).astype(jnp.int32)
            index_y = ((number // BOXES_Z) % BOXES_Y).astype(jnp.int32)
            index_z = (number % BOXES_Z).astype(jnp.int32)
            starts = (jnp.zeros((), jnp.int32), (index_x * BOX_X).astype(jnp.int32), (index_y * BOX_Y).astype(jnp.int32), (index_z * BOX_Z).astype(jnp.int32))
            window = lax.dynamic_slice(padded, starts, (FIELDS, BOX_X + 2, BOX_Y + 2, BOX_Z + 2))
            slab_y, slab_z = coarse_slabs(window, lead_y, span_y, lead_z, span_z)
            return slab_faces(slab_y, slab_z)

        faces_y, faces_z = lax.map(box_faces, jnp.arange(total_boxes, dtype=jnp.int32))
        faces_y = faces_y.reshape((BOXES_X, BOXES_Y, BOXES_Z) + faces_y.shape[1:])[fine_owner, rows_y, rows_z]
        faces_z = faces_z.reshape((BOXES_X, BOXES_Y, BOXES_Z) + faces_z.shape[1:])[fine_owner, rows_y, rows_z]
        fine_boxes = split_boxes(fine_state, fine_x, BOX_Y, BOX_Z)
        left_cells = jnp.roll(fine_boxes, 1, axis=0)[:, :, :, :, -1:]
        right_cells = jnp.roll(fine_boxes, -1, axis=0)[:, :, :, :, :1]
        widened = jnp.concatenate((left_cells, fine_boxes, right_cells), axis=4)
        widened = widened.reshape((total_boxes,) + widened.shape[3:])
        faces_y = faces_y.reshape((total_boxes,) + faces_y.shape[3:])
        faces_z = faces_z.reshape((total_boxes,) + faces_z.shape[3:])

        def fine_rate_of(inputs):
            return tendency(fine_padded(inputs[0], inputs[1], inputs[2]), inputs[3])

        rates = lax.map(fine_rate_of, (widened, faces_y, faces_z, wind_boxes))
        rates = join_boxes(rates.reshape((BOXES_X, BOXES_Y, BOXES_Z) + rates.shape[1:]))
        coarse_state = coarse_fields + fraction * coarse_rate
        fine_state = fine_fields + fraction * rates
    fine_boxes = split_boxes(fine_state, fine_x, BOX_Y, BOX_Z)
    averaged = jax.vmap(jax.vmap(jax.vmap(coarsen)))(fine_boxes)
    placed = jnp.zeros_like(averaged).at[fine_owner, rows_y, rows_z].set(averaged)
    coarse_boxes = split_boxes(coarse_state, BOX_X, BOX_Y, BOX_Z)
    coarse_boxes = coarse_boxes.at[:, :, :, :, :, lead_y:lead_y + span_y, lead_z:lead_z + span_z].set(placed)
    return join_boxes(coarse_boxes), fine_state
```

```python
import functools

import jax
import jax.numpy as jnp
from jax import lax
from jax.experimental import pallas as pl
from jax.experimental.pallas import tpu as pltpu
from jax.sharding import PartitionSpec as P

MESH = pl.DeviceIdType.MESH
F32 = jnp.float32
BF16 = jnp.bfloat16
diffusion = 0.05
section_weights = (1.0 / 3.0, 0.5, 1.0)

RING_X, RING_Z = 4, 8
BOXES = RING_X * RING_Z
FIELDS, CX, FX, NY, LANES = 4, 16, 32, 16, 128
LOW, TOP = 8, 24
PAY = 88
EDGE = 24
CHUNKS = 4
CHUNK_ROWS = 256 // CHUNKS
COPIES = 160


def split_dot(value, weights):
    high = value.astype(BF16)
    rest = value - high.astype(F32)
    mid = rest.astype(BF16)
    low = (rest - mid.astype(F32)).astype(BF16)
    out = jnp.dot(low, weights, preferred_element_type=F32)
    out = out + jnp.dot(mid, weights, preferred_element_type=F32)
    return out + jnp.dot(high, weights, preferred_element_type=F32)


def refine_weights():
    row = lax.broadcasted_iota(jnp.int32, (256, 256), 0)
    col = lax.broadcasted_iota(jnp.int32, (256, 256), 1)
    side, cell, odd = col // 128, (col % 128) // 2, col % 2
    main = (row < 128) & (row // 64 == side)
    near = main & (row % 64 == cell)
    far = main & (row % 64 == cell + 2 * odd - 1)
    extra = row - 128
    corner = (extra >= 0) & (extra < 4) & (extra // 2 == side)
    corner = corner & (col % 128 == jnp.where(extra % 2 == 0, 0, 127))
    return jnp.where(near, 0.75, jnp.where(far | corner, 0.25, 0.0)).astype(BF16)


def average_weights():
    row = lax.broadcasted_iota(jnp.int32, (256, 128), 0)
    col = lax.broadcasted_iota(jnp.int32, (256, 128), 1)
    hit = (row // 128 == col // 64) & ((row % 128) // 2 == col % 64)
    return jnp.where(hit, 0.125, 0.0).astype(BF16)


def interleave_weights():
    row = lax.broadcasted_iota(jnp.int32, (128, 128), 0)
    col = lax.broadcasted_iota(jnp.int32, (128, 128), 1)
    return jnp.where(col == 2 * (row % 64) + row // 64, 1.0, 0.0).astype(BF16)


def coefficients(wind, fraction):
    weight = (0.5 * fraction) * wind
    base = diffusion * fraction
    return base - weight, base + weight


def stepped(state, at, field, base, ghost, coefs, fraction, lane):
    q = state[at, field, LOW:TOP, :]
    behind = state[at - 1, field, LOW:TOP, :]
    ahead = state[at + 1, field, LOW:TOP, :]
    below = state[at, field, LOW - 1 : TOP - 1, :]
    above = state[at, field, LOW + 1 : TOP + 1, :]
    under = pltpu.roll(jnp.where(lane == 127, ghost, q), 1, 1)
    over = pltpu.roll(jnp.where(lane == 0, ghost, q), 127, 1)
    (xp, xm), (yp, ym), (zp, zm) = coefs
    total = (xp * ahead + xm * behind) + (yp * above + ym * below) + (zp * over + zm * under)
    return total + (base - (6.0 * diffusion * fraction) * q)


def kernel(
    cf, cw, ff, fw, own, co, fo,
    sc0, sc1, sc2, sc3, wc, sf0, sf1, sf2, sf3, wf,
    ysend, yrecv, zsend, zrecv, pays, paysel, payzs, slab, corner, face, zt, zface,
    pairs, avg0s, avgzs, result, w_face, w_avg, w_mix,
    send_sem, recv_sem, load_sem,
):
    gx, gy, gz = lax.axis_index("gx"), lax.axis_index("gy"), lax.axis_index("gz")
    tz, tx = gx // RING_X, gx % RING_X

    def along_x(step):
        return (tz * RING_X + (tx + step + RING_X) % RING_X, gy, gz)

    def along_z(step):
        return (((tz + step + RING_Z) % RING_Z) * RING_X + tx, gy, gz)

    def along_row(step):
        return ((gx + step + BOXES) % BOXES, gy, gz)

    def along_y(step):
        return (gx, (gy + step + 4) % 4, gz)

    other_z = (gx, gy, 1 - gz)

    sent = []

    def ship(src, dst, device):
        at = len(sent)
        copy = pltpu.make_async_remote_copy(
            src_ref=src, dst_ref=dst, send_sem=send_sem.at[at], recv_sem=recv_sem.at[at],
            device_id=device, device_id_type=MESH,
        )
        copy.start()
        sent.append(copy)
        return copy

    loads = []

    def load(src, dst):
        copy = pltpu.make_async_copy(src, dst, load_sem.at[len(loads)])
        copy.start()
        loads.append(copy)
        return copy

    in_cf = [load(cf.at[f], sc0.at[pl.ds(1, CX), f, pl.ds(LOW, NY), :]) for f in range(FIELDS)]
    in_ff = [load(ff.at[f], sf0.at[pl.ds(1, FX), f, pl.ds(LOW, NY), :]) for f in range(FIELDS)]
    in_cw = load(cw, wc)
    in_fw = load(fw, wf)

    barrier = pltpu.get_barrier_semaphore()
    partners = [along_x(s) for s in (-1, 1, 2)] + [along_z(s) for s in (-2, -1, 1, 2)]
    partners += [along_row(-1), along_row(1), along_y(-1), along_y(1), other_z]
    for partner in partners:
        pl.semaphore_signal(barrier, inc=1, device_id=partner, device_id_type=MESH)

    lane = lax.broadcasted_iota(jnp.int32, (NY, LANES), 1)
    lane8 = lax.broadcasted_iota(jnp.int32, (8, LANES), 1)
    w_face[...] = refine_weights()
    w_avg[...] = average_weights()
    w_mix[...] = interleave_weights()

    shift = (own[0] - gx + BOXES) % BOXES
    back = (BOXES - shift) % BOXES
    shift_x = shift % RING_X
    shift_z = (shift // RING_X + (tx + shift_x) // RING_X) % RING_Z
    back_x = back % RING_X
    back_z = (back // RING_X + (tx + back_x) // RING_X) % RING_Z

    pl.semaphore_wait(barrier, len(partners))

    coarse = [sc0, sc1, sc2]
    fine = [sf0, sf1, sf2]
    halo = {}

    def coarse_x_halo(k):
        s = coarse[k]
        a = ship(s.at[CX, :, pl.ds(LOW, NY), :], s.at[0, :, pl.ds(LOW, NY), :], along_row(1))
        b = ship(s.at[1, :, pl.ds(LOW, NY), :], s.at[CX + 1, :, pl.ds(LOW, NY), :], along_row(-1))
        halo["cx", k] = (a, b)

    def fine_x_halo(k):
        s = fine[k]
        a = ship(s.at[FX, :, pl.ds(LOW, NY), :], s.at[0, :, pl.ds(LOW, NY), :], along_row(1))
        b = ship(s.at[1, :, pl.ds(LOW, NY), :], s.at[FX + 1, :, pl.ds(LOW, NY), :], along_row(-1))
        halo["fx", k] = (a, b)

    def pack(k):
        s = coarse[k]
        edge_lane = jnp.where(gz == 0, 127, 0)

        def group(g, carry):
            acc_z, acc_t, acc_c = carry
            lows, highs = [], []
            for h in range(2):
                x = 2 * g + h + 1
                ysend[k, 0, g, 4 * h : 4 * h + 4, :] = s[x, :, LOW, :]
                ysend[k, 1, g, 4 * h : 4 * h + 4, :] = s[x, :, TOP - 1, :]
                lows.append(0.75 * s[x, :, LOW + 3, :] + 0.25 * s[x, :, LOW + 4, :])
                highs.append(0.25 * s[x, :, LOW + 11, :] + 0.75 * s[x, :, LOW + 12, :])
                for f in range(FIELDS):
                    p = 8 * g + 4 * h + f
                    q = s[x, f, LOW:TOP, :]
                    moved = pltpu.roll(q, (2 * p + gz - edge_lane + 128) % 128, 1)
                    acc_z = jnp.where(lane == 2 * p + gz, moved, acc_z)
                    after = pltpu.roll(q, 127, 1)
                    t = jnp.where(lane < 64, 0.75 * q + 0.25 * after, 0.25 * q + 0.75 * after)
                    t = pltpu.roll(t, (p - 31 + 128) % 128, 1)
                    acc_t = jnp.where(lane % 64 == p, t, acc_t)
            low = jnp.concatenate(lows, axis=0)
            high = jnp.concatenate(highs, axis=0)
            row = pl.multiple_of(8 * g, 8)
            pays[k][0, pl.ds(row, 8), :] = jnp.where(
                lane8 < 64, pltpu.roll(low, 96, 1), pltpu.roll(high, 32, 1)
            )
            for n, (value, source) in enumerate(((low, 31), (low, 96), (high, 31), (high, 96))):
                moved = pltpu.roll(value, (4 * g + n - source + 128) % 128, 1)
                acc_c = jnp.where(lane8 == 4 * g + n, moved, acc_c)
            return acc_z, acc_t, acc_c

        zero = jnp.zeros((NY, LANES), F32)
        acc_z, acc_t, acc_c = lax.fori_loop(
            0, 8, group, (zero, zero, jnp.zeros((8, LANES), F32))
        )
        zsend[k] = acc_z
        pays[k][0, 64:80, :] = acc_t
        pays[k][0, 80:88, :] = acc_c
        halo["cy", k] = (
            ship(ysend.at[k, 1], yrecv.at[k, 0], along_y(1)),
            ship(ysend.at[k, 0], yrecv.at[k, 1], along_y(-1)),
        )
        halo["cz", k] = (ship(zsend.at[k], zrecv.at[k], other_z),)

    def wait(*names):
        for name in names:
            for copy in halo.pop(name):
                copy.wait_recv()

    def forward_x(k):
        src = pays[k].at[0]
        halo["px", k] = tuple(
            ship(src, pays[k].at[slot], along_x(-slot)) for slot in (1, 2, 3)
        )

    def forward_z1(k):
        wait(("px", k))
        paysel[k] = pays[k][shift_x]
        payzs[k][0] = paysel[k]
        halo["pz1", k] = tuple(
            ship(paysel.at[k], payzs[k].at[slot], along_z(-step))
            for slot, step in ((2, 2), (6, -2), (1, 1), (7, -1))
        )

    def forward_z2(k):
        copies = halo.pop(("pz1", k))
        halo["pz1", k] = copies[2:]
        for copy in copies[:2]:
            copy.wait_recv()
        half = PAY // 2 + 4
        first, second = pl.ds(0, half), pl.ds(half, PAY - half)
        halo["pz2", k] = (
            ship(payzs[k].at[2, first], payzs[k].at[4, first], along_z(-2)),
            ship(payzs[k].at[6, second], payzs[k].at[4, second], along_z(2)),
            ship(payzs[k].at[2], payzs[k].at[3], along_z(-1)),
            ship(payzs[k].at[6], payzs[k].at[5], along_z(1)),
        )

    def arrive(k):
        wait(("pz1", k), ("pz2", k))
        slab[k, 8:72, :] = payzs[k][shift_z, 0:64, :]
        slab[k, 80:104, :] = payzs[k][shift_z, 64:88, :]
        s = slab.at[k]
        halo["edge", k] = (
            ship(s.at[pl.ds(64, 8)], s.at[pl.ds(0, 8)], along_row(1)),
            ship(s.at[pl.ds(80, EDGE)], s.at[pl.ds(104, EDGE)], along_row(1)),
            ship(s.at[pl.ds(8, 8)], s.at[pl.ds(72, 8)], along_row(-1)),
            ship(s.at[pl.ds(80, EDGE)], s.at[pl.ds(128, EDGE)], along_row(-1)),
        )

    def faces(k):
        wait(("edge", k))
        s = slab.at[k]
        cols = s[96:104, :]
        for g in range(8):
            corner[8 + 8 * g : 16 + 8 * g, :] = pltpu.roll(cols, (128 - 4 * g) % 128, 1)
        corner[0:8, :] = pltpu.roll(s[120:128, :], 100, 1)
        corner[72:80, :] = s[144:152, :]
        parts = []
        for ref in (s, corner):
            before, here, after = ref[4:68, :], ref[8:72, :], ref[12:76, :]
            even = 0.25 * before + 0.75 * here
            odd = 0.75 * here + 0.25 * after
            parts.append(jnp.concatenate((even, odd), axis=0))
        wide = jnp.concatenate(parts, axis=1)
        made = split_dot(wide, w_face[...])
        face[...] = made.reshape(16, 8, 256)
        state = fine[k]

        def place(g, carry):
            for o in range(2):
                rows = face[8 * o + g]
                for h in range(2):
                    x = 4 * g + 2 * h + o + 1
                    state[x, :, LOW - 1, :] = rows[4 * h : 4 * h + 4, 0:128]
                    state[x, :, TOP, :] = rows[4 * h : 4 * h + 4, 128:256]
            return carry

        lax.fori_loop(0, 8, place, 0)

        own_z, left, right = s[80:96, :], s[104:120, :], s[128:144, :]
        before = jnp.where(lane % 64 < 4, pltpu.roll(left, 68, 1), pltpu.roll(own_z, 4, 1))
        after = jnp.where(lane % 64 >= 60, pltpu.roll(right, 60, 1), pltpu.roll(own_z, 124, 1))
        zt[0] = 0.25 * before + 0.75 * own_z
        zt[1] = 0.75 * own_z + 0.25 * after
        for o in range(2):
            near = zt[o, 4:12, :]
            zface[o, pl.ds(0, 8, stride=2), :] = 0.25 * zt[o, 3:11, :] + 0.75 * near
            zface[o, pl.ds(1, 8, stride=2), :] = 0.75 * near + 0.25 * zt[o, 5:13, :]
        both = zface[...].reshape(32, LANES)
        zface[...] = split_dot(both, w_mix[...]).reshape(2, NY, LANES)

    def coarse_plane(k, x):
        fraction = section_weights[k]
        s = coarse[k]
        coefs = [coefficients(wc[d, x], fraction) for d in range(3)]
        column = zrecv[k]
        for f in range(FIELDS):
            ghost = pltpu.roll(column, (127 - 2 * (FIELDS * x + f) + 128) % 128, 1)
            base = sc0[x + 1, f, LOW:TOP, :]
            new = stepped(s, x + 1, f, base, ghost, coefs, fraction, lane)
            if k == 2:
                sc3[f, x] = new
            else:
                coarse[k + 1][x + 1, f, LOW:TOP, :] = new

    def coarse_section(k):
        s = coarse[k]
        wait(("cy", k), ("cz", k))

        def place(g, carry):
            for h in range(2):
                s[2 * g + h + 1, :, LOW - 1, :] = yrecv[k, 0, g, 4 * h : 4 * h + 4, :]
                s[2 * g + h + 1, :, TOP, :] = yrecv[k, 1, g, 4 * h : 4 * h + 4, :]
            return carry

        lax.fori_loop(0, 8, place, 0)

        def inner(x, carry):
            coarse_plane(k, x)
            return carry

        lax.fori_loop(1, CX - 1, inner, 0)
        wait(("cx", k))
        coarse_plane(k, jnp.int32(0))
        coarse_plane(k, jnp.int32(CX - 1))
        if k < 2:
            coarse_x_halo(k + 1)

    def fine_plane(k, j, o):
        fraction = section_weights[k]
        s = fine[k]
        x = 2 * j + o
        coefs = [coefficients(wf[d, x], fraction) for d in range(3)]
        column = zface[o]
        made = []
        for f in range(FIELDS):
            ghost = pltpu.roll(column, (127 - 2 * (FIELDS * j + f) + 128) % 128, 1)
            base = sf0[x + 1, f, LOW:TOP, :]
            new = stepped(s, x + 1, f, base, ghost, coefs, fraction, lane)
            made.append(new)
            if k == 2:
                sf3[f, x] = new
            else:
                fine[k + 1][x + 1, f, LOW:TOP, :] = new
        return made

    def fine_section(k):
        wait(("fx", k))

        def pair(j, carry):
            fine_plane(k, j, 0)
            fine_plane(k, j, 1)
            return carry

        pair(jnp.int32(0), 0)
        pair(jnp.int32(15), 0)
        fine_x_halo(k + 1)
        lax.fori_loop(1, 15, pair, 0)

    def last_section():
        wait(("fx", 2))

        def pair(j, carry):
            first = fine_plane(2, j, 0)
            second = fine_plane(2, j, 1)
            for f in range(FIELDS):
                pairs[j, f] = first[f] + second[f]
            return carry

        for c in range(CHUNKS):
            j0 = c * (16 // CHUNKS)
            lax.fori_loop(j0, j0 + 16 // CHUNKS, pair, 0)
            rows = []
            for j in range(j0, j0 + 16 // CHUNKS):
                for fp in range(2):
                    halves = [
                        pairs[j, 2 * fp + n, pl.ds(0, 8, stride=2), :]
                        + pairs[j, 2 * fp + n, pl.ds(1, 8, stride=2), :]
                        for n in range(2)
                    ]
                    rows.append(jnp.concatenate(halves, axis=1))
            avg0s[c][0] = split_dot(jnp.concatenate(rows, axis=0), w_avg[...])
            src = avg0s[c].at[0]
            halo["ax1", c] = (
                ship(src, avg0s[c].at[3], along_x(1)),
                ship(src, avg0s[c].at[1], along_x(-1)),
            )

    def average_x2(c):
        wait(("ax1", c))
        first, second = pl.ds(0, CHUNK_ROWS // 2), pl.ds(CHUNK_ROWS // 2, CHUNK_ROWS // 2)
        halo["ax2", c] = (
            ship(avg0s[c].at[3, first], avg0s[c].at[2, first], along_x(1)),
            ship(avg0s[c].at[1, second], avg0s[c].at[2, second], along_x(-1)),
        )

    def average_z(c, step):
        if step == 1:
            wait(("ax2", c))
            avgzs[c][0] = avg0s[c][back_x]
        else:
            wait(("az", c, step - 1))
        up, down = (RING_Z - step + 1) % RING_Z, step - 1
        if step < 4:
            halo["az", c, step] = (
                ship(avgzs[c].at[up], avgzs[c].at[up - 1 if up else 7], along_z(1)),
                ship(avgzs[c].at[down], avgzs[c].at[down + 1], along_z(-1)),
            )
        else:
            half = CHUNK_ROWS // 2
            first, second = pl.ds(0, half), pl.ds(half, half)
            halo["az", c, step] = (
                ship(avgzs[c].at[5, first], avgzs[c].at[4, first], along_z(1)),
                ship(avgzs[c].at[3, second], avgzs[c].at[4, second], along_z(-1)),
            )

    inside = (lane8 >= 32) & (lane8 < 96)

    def average_done(c):
        wait(("az", c, 4))
        result[...] = avgzs[c][back_z].reshape(CHUNK_ROWS // 8, 8, LANES)
        for j in range(16 // CHUNKS):
            x = c * (16 // CHUNKS) + j
            for fp in range(2):
                block = result[2 * j + fp]
                for n in range(2):
                    f = 2 * fp + n
                    moved = pltpu.roll(block, 32 if n == 0 else 96, 1)
                    sc3[f, x, 4:12, :] = jnp.where(inside, moved, sc3[f, x, 4:12, :])

    for copy in in_cf:
        copy.wait()
    coarse_x_halo(0)
    pack(0)
    forward_x(0)
    for copy in in_ff:
        copy.wait()
    fine_x_halo(0)
    in_cw.wait()
    coarse_section(0)
    pack(1)
    forward_x(1)
    forward_z1(0)
    coarse_section(1)
    pack(2)
    forward_x(2)
    forward_z2(0)
    forward_z1(1)
    arrive(0)
    forward_z1(2)
    forward_z2(1)
    in_fw.wait()
    faces(0)
    fine_section(0)
    forward_z2(2)
    arrive(1)
    coarse_section(2)
    faces(1)
    fine_section(1)
    arrive(2)
    faces(2)
    last_section()
    out_fine = load(sf3, fo)
    for c in range(CHUNKS):
        average_x2(c)
    for step in (1, 2, 3, 4):
        for c in range(CHUNKS):
            average_z(c, step)
    for c in range(CHUNKS):
        average_done(c)
    out_coarse = load(sc3, co)
    for copy in sent:
        copy.wait_send()
    out_fine.wait()
    out_coarse.wait()


def shards(coarse_fields, coarse_wind, fine_fields, fine_wind, fine_owner):
    anywhere = pl.BlockSpec(memory_space=pl.ANY)
    vmem = lambda *shape: pltpu.VMEM(shape, F32)
    scratch = (
        [vmem(CX + 2, FIELDS, 32, LANES)] * 3
        + [vmem(FIELDS, CX, NY, LANES), vmem(3, CX, NY, LANES)]
        + [vmem(FX + 2, FIELDS, 32, LANES)] * 3
        + [vmem(FIELDS, FX, NY, LANES), vmem(3, FX, NY, LANES)]
        + [
            vmem(3, 2, 8, 8, LANES), vmem(3, 2, 8, 8, LANES),
            vmem(3, NY, LANES), vmem(3, NY, LANES),
            [vmem(RING_X, PAY, LANES)] * 3, vmem(3, PAY, LANES), [vmem(RING_Z, PAY, LANES)] * 3,
            vmem(3, 152, LANES), vmem(80, LANES), vmem(16, 8, 256),
            vmem(2, NY, LANES), vmem(2, NY, LANES),
            vmem(CX, FIELDS, NY, LANES),
            [vmem(RING_X, CHUNK_ROWS, LANES)] * CHUNKS,
            [vmem(RING_Z, CHUNK_ROWS, LANES)] * CHUNKS,
            vmem(CHUNK_ROWS // 8, 8, LANES),
            pltpu.VMEM((256, 256), BF16), pltpu.VMEM((256, 128), BF16),
            pltpu.VMEM((128, 128), BF16),
            pltpu.SemaphoreType.DMA((COPIES,)), pltpu.SemaphoreType.DMA((COPIES,)),
            pltpu.SemaphoreType.DMA((16,)),
        ]
    )
    return pl.pallas_call(
        kernel,
        out_shape=(
            jax.ShapeDtypeStruct(coarse_fields.shape, F32),
            jax.ShapeDtypeStruct(fine_fields.shape, F32),
        ),
        in_specs=[anywhere] * 4 + [pl.BlockSpec(memory_space=pltpu.SMEM)],
        out_specs=(anywhere, anywhere),
        scratch_shapes=scratch,
        compiler_params=pltpu.CompilerParams(
            collective_id=0, has_side_effects=True, vmem_limit_bytes=48 * 1024 * 1024
        ),
        name="two_level_step",
    )(coarse_fields, coarse_wind, fine_fields, fine_wind, fine_owner.reshape((1,)))


def solution(mesh):
    spec = P(None, "gx", "gy", "gz")
    return jax.shard_map(
        shards,
        mesh=mesh,
        in_specs=(spec, spec, spec, spec, P("gx", "gy", "gz")),
        out_specs=(spec, spec),
        check_vma=False,
    )
```

```python
import functools

import jax
import jax.numpy as jnp
from jax import lax
from jax.experimental import pallas as pl
from jax.experimental.pallas import tpu as pltpu
from jax.sharding import PartitionSpec as P

MESH = pl.DeviceIdType.MESH
F32 = jnp.float32
BF16 = jnp.bfloat16
diffusion = 0.05
section_weights = (1.0 / 3.0, 0.5, 1.0)

RING_X, RING_Z = 4, 8
BOXES = RING_X * RING_Z
FIELDS, CX, FX, NY, LANES = 4, 16, 32, 16, 128
LOW, TOP = 8, 24
PAY = 104
CHUNKS = 4
CHUNK_ROWS = 256 // CHUNKS
COPIES = 72
STRIDES = (1, 3)


def split_dot(value, weights):
    high = value.astype(BF16)
    rest = value - high.astype(F32)
    mid = rest.astype(BF16)
    low = (rest - mid.astype(F32)).astype(BF16)
    out = jnp.dot(low, weights, preferred_element_type=F32)
    out = out + jnp.dot(mid, weights, preferred_element_type=F32)
    return out + jnp.dot(high, weights, preferred_element_type=F32)


def refine_weights():
    row = lax.broadcasted_iota(jnp.int32, (256, 256), 0)
    col = lax.broadcasted_iota(jnp.int32, (256, 256), 1)
    side, cell, odd = col // 128, (col % 128) // 2, col % 2
    main = (row < 128) & (row // 64 == side)
    near = main & (row % 64 == cell)
    far = main & (row % 64 == cell + 2 * odd - 1)
    extra = row - 128
    corner = (extra >= 0) & (extra < 4) & (extra // 2 == side)
    corner = corner & (col % 128 == jnp.where(extra % 2 == 0, 0, 127))
    return jnp.where(near, 0.75, jnp.where(far | corner, 0.25, 0.0)).astype(BF16)


def average_weights():
    row = lax.broadcasted_iota(jnp.int32, (256, 128), 0)
    col = lax.broadcasted_iota(jnp.int32, (256, 128), 1)
    hit = (row // 128 == col // 64) & ((row % 128) // 2 == col % 64)
    return jnp.where(hit, 0.125, 0.0).astype(BF16)


def interleave_weights():
    row = lax.broadcasted_iota(jnp.int32, (256, 256), 0)
    col = lax.broadcasted_iota(jnp.int32, (256, 256), 1)
    side, p = row // 128, row % 128
    inner = (p >= 8) & (p < 72) & (col == 2 * (p - 8) + side)
    before = (p >= 4) & (p < 8) & (col == 128 + 2 * (p - 4) + side)
    after = (p >= 72) & (p < 76) & (col == 136 + 2 * (p - 72) + side)
    return jnp.where(inner | before | after, 1.0, 0.0).astype(BF16)


def coefficients(wind, fraction):
    weight = (0.5 * fraction) * wind
    base = diffusion * fraction
    return base - weight, base + weight


def stepped(state, field, at, base, ghost, coefs, fraction, lane):
    q = state[field, at, LOW:TOP, :]
    behind = state[field, at - 1, LOW:TOP, :]
    ahead = state[field, at + 1, LOW:TOP, :]
    below = state[field, at, LOW - 1 : TOP - 1, :]
    above = state[field, at, LOW + 1 : TOP + 1, :]
    low_side = q if ghost is None else jnp.where(lane == 127, ghost, q)
    top_side = q if ghost is None else jnp.where(lane == 0, ghost, q)
    under = pltpu.roll(low_side, 1, 1)
    over = pltpu.roll(top_side, 127, 1)
    (xp, xm), (yp, ym), (zp, zm) = coefs
    total = (xp * ahead + xm * behind) + (yp * above + ym * below) + (zp * over + zm * under)
    return total + (base - (6.0 * diffusion * fraction) * q)


def kernel(
    cf, cw, ff, fw, own, co, fo,
    tc0, tc1, tc2, uc1, uc2, sc3, wc, sf0, sf1, sf2, sf3, wf,
    ysend, yrecv, zsend, zrecv, payxs, payzs, slab, corner, face, zt, zface,
    pairs, avgxs, avgzs, result, w_face, w_avg, w_mix,
    send_sem, recv_sem, load_sem,
):
    gx, gy, gz = lax.axis_index("gx"), lax.axis_index("gy"), lax.axis_index("gz")
    tz, tx = gx // RING_X, gx % RING_X

    def along_x(step):
        return (tz * RING_X + (tx + step + RING_X) % RING_X, gy, gz)

    def along_z(step):
        return (((tz + step + RING_Z) % RING_Z) * RING_X + tx, gy, gz)

    def along_row(step):
        return ((gx + step + BOXES) % BOXES, gy, gz)

    def along_y(step):
        return (gx, (gy + step + 4) % 4, gz)

    other_z = (gx, gy, 1 - gz)

    sent = []
    halo = {}

    def ship(src, dst, device):
        at = len(sent)
        copy = pltpu.make_async_remote_copy(
            src_ref=src, dst_ref=dst, send_sem=send_sem.at[at], recv_sem=recv_sem.at[at],
            device_id=device, device_id_type=MESH,
        )
        copy.start()
        sent.append(copy)
        return copy

    def wait(*names):
        for name in names:
            for copy in halo.pop(name):
                copy.wait_recv()

    loads = []

    def load(src, dst):
        copy = pltpu.make_async_copy(src, dst, load_sem.at[len(loads)])
        copy.start()
        loads.append(copy)
        return copy

    rows = pl.ds(LOW, NY)
    in_cf = load(cf, tc0.at[:, pl.ds(3, CX), rows, :])
    in_cw = load(cw, wc.at[:, pl.ds(2, CX)])
    in_ff = load(ff, sf0.at[:, pl.ds(3, FX), rows, :])
    in_fw = load(fw, wf.at[:, pl.ds(2, FX)])

    barrier = pltpu.get_barrier_semaphore()
    partners = [along_row(-1), along_row(1), along_y(-1), along_y(1), other_z]
    partners += [along_x(s) for s in (-1, 1, 2)] + [along_z(s) for s in (-3, -1, 1, 3)]
    for partner in partners:
        pl.semaphore_signal(barrier, inc=1, device_id=partner, device_id_type=MESH)

    lane = lax.broadcasted_iota(jnp.int32, (NY, LANES), 1)
    lane8 = lax.broadcasted_iota(jnp.int32, (8, LANES), 1)

    def parts_of(shift):
        part_x = shift % RING_X
        part_z = (shift // RING_X + (tx + part_x) // RING_X) % RING_Z
        signed = part_z - jnp.where(part_z > 4, RING_Z, 0)
        third = (signed + 4) // 3
        return part_x, signed - 3 * third + 4, third

    shift = (own[0] - gx + BOXES) % BOXES
    there = parts_of(shift)
    home = parts_of((BOXES - shift) % BOXES)

    def start_halos():
        def both(name, src, dst, first, last, width, end, where):
            halo[name] = (
                ship(src.at[:, pl.ds(last, width)], where(dst, 0, width), along_row(1)),
                ship(src.at[:, pl.ds(first, width)], where(dst, end, width), along_row(-1)),
            )

        padded = lambda ref, at, width: ref.at[:, pl.ds(at, width), rows, :]
        plain = lambda ref, at, width: ref.at[:, pl.ds(at, width)]
        both("cf", cf, tc0, 0, CX - 3, 3, CX + 3, padded)
        both("cw", cw, wc, 0, CX - 2, 2, CX + 2, plain)
        both("ff", ff, sf0, 0, FX - 3, 3, FX + 3, padded)
        both("fw", fw, wf, 0, FX - 2, 2, FX + 2, plain)

    slabs = [tc0, tc1, tc2]

    def slab_range(k, first, last):
        fraction = section_weights[k]

        def inner(at, carry):
            coefs = [coefficients(wc[d, at - 1], fraction) for d in range(3)]
            for f in range(FIELDS):
                base = tc0[f, at, rows, :]
                new = stepped(slabs[k], f, at, base, None, coefs, fraction, lane)
                slabs[k + 1][f, at, rows, :] = new
            return carry

        lax.fori_loop(first + 3, last + 3, inner, 0)

    def pack_start():
        zero = jnp.zeros((NY, LANES), F32)
        return zero, zero, jnp.zeros((8, LANES), F32)

    def pack_group(k, g, carry):
        s = slabs[k]
        low_z, high_z, ends = carry
        lows, highs = [], []
        for h in range(2):
            at = 2 * g + h + 1
            lows.append(0.75 * s[:, at, LOW + 3, :] + 0.25 * s[:, at, LOW + 4, :])
            highs.append(0.25 * s[:, at, LOW + 11, :] + 0.75 * s[:, at, LOW + 12, :])
            for f in range(FIELDS):
                p = 8 * g + 4 * h + f
                q = s[f, at, rows, :]
                after = pltpu.roll(q, 127, 1)
                t = jnp.where(lane < 64, 0.75 * q + 0.25 * after, 0.25 * q + 0.75 * after)
                low_z = jnp.where(lane == p, pltpu.roll(t, (p - 31 + 128) % 128, 1), low_z)
                high_z = jnp.where(lane == p, pltpu.roll(t, (p - 95 + 128) % 128, 1), high_z)
        low = jnp.concatenate(lows, axis=0)
        high = jnp.concatenate(highs, axis=0)
        row = pl.multiple_of(8 * g, 8)
        payxs[k][0, pl.ds(row, 8), :] = jnp.where(
            lane8 < 64, pltpu.roll(low, 96, 1), pltpu.roll(high, 32, 1)
        )
        for n, (value, source) in enumerate(((low, 31), (low, 96), (high, 31), (high, 96))):
            to = 80 + 4 * g + n
            ends = jnp.where(lane8 == to, pltpu.roll(value, (to - source + 128) % 128, 1), ends)
        return low_z, high_z, ends

    def pack_range(k, first, last, carry):
        return lax.fori_loop(first, last, functools.partial(pack_group, k), carry)

    def pack_end(k, carry):
        low_z, high_z, ends = carry
        payxs[k][0, 80:88, :] = jnp.where(lane8 >= 80, ends, low_z[3:11, :])
        payxs[k][0, 88:90, :] = low_z[11:13, :]
        payxs[k][0, 92:102, :] = high_z[3:13, :]

    def shift_x(name, bufs):
        halo[name, 0] = tuple(
            ship(bufs.at[0], bufs.at[slot], along_x(-slot)) for slot in (1, 2, 3)
        )

    def faces(k):
        wait((("pay", k), 2))
        slab[...] = payzs[k][1][there[2]]
        cols = slab[80:88, :]
        for g in range(10):
            corner[8 * g : 8 * g + 8, :] = pltpu.roll(cols, (48 - 4 * g + 128) % 128, 1)
        parts = []
        for ref in (slab, corner):
            before, here, after = ref[0:72, :], ref[4:76, :], ref[8:80, :]
            even = 0.25 * before + 0.75 * here
            odd = 0.75 * here + 0.25 * after
            parts.append(jnp.concatenate((even, odd), axis=0))
        made = split_dot(jnp.concatenate(parts, axis=1), w_face[...])
        face[...] = made.reshape(18, 8, 256)
        state = fine[k]

        def place(m, carry):
            for o in range(2):
                block = face[9 * o + m]
                for h in range(2):
                    at = 4 * m + 2 * h + o + 1
                    state[:, at, LOW - 1, :] = block[4 * h : 4 * h + 4, 0:128]
                    state[:, at, TOP, :] = block[4 * h : 4 * h + 4, 128:256]
            return carry

        lax.fori_loop(0, 9, place, 0)

        for side, first in enumerate((80, 92)):
            v = slab[first : first + 10, :]
            even = 0.25 * pltpu.roll(v, 4, 1) + 0.75 * v
            odd = 0.75 * v + 0.25 * pltpu.roll(v, 124, 1)
            for o, w in enumerate((even, odd)):
                near = 0.75 * w[1:9, :]
                zt[o, side, pl.ds(0, 8, stride=2), :] = 0.25 * w[0:8, :] + near
                zt[o, side, pl.ds(1, 8, stride=2), :] = near + 0.25 * w[2:10, :]
        both = jnp.concatenate(
            [jnp.concatenate((zt[o, 0], zt[o, 1]), axis=1) for o in range(2)], axis=0
        )
        zface[...] = split_dot(both, w_mix[...]).reshape(2, NY, 256)

    def send_edges(k):
        s, off = ((tc0, 3), (uc1, 1), (uc2, 1))[k]
        edge_lane = jnp.where(gz == 0, 127, 0)

        def group(g, acc):
            for h in range(2):
                at = 2 * g + h + off
                ysend[k, 0, g, 4 * h : 4 * h + 4, :] = s[:, at, LOW, :]
                ysend[k, 1, g, 4 * h : 4 * h + 4, :] = s[:, at, TOP - 1, :]
                for f in range(FIELDS):
                    to = 2 * (8 * g + 4 * h + f) + gz
                    moved = pltpu.roll(s[f, at, rows, :], (to - edge_lane + 128) % 128, 1)
                    acc = jnp.where(lane == to, moved, acc)
            return acc

        zsend[k] = lax.fori_loop(0, 8, group, jnp.zeros((NY, LANES), F32))
        copies = [
            ship(ysend.at[k, 1], yrecv.at[k, 0], along_y(1)),
            ship(ysend.at[k, 0], yrecv.at[k, 1], along_y(-1)),
            ship(zsend.at[k], zrecv.at[k], other_z),
        ]
        if k:
            copies += [
                ship(s.at[:, CX, rows, :], s.at[:, 0, rows, :], along_row(1)),
                ship(s.at[:, 1, rows, :], s.at[:, CX + 1, rows, :], along_row(-1)),
            ]
        halo["edges", k] = copies

    def coarse_section(k):
        s, off = ((tc0, 3), (uc1, 1), (uc2, 1))[k]
        fraction = section_weights[k]
        wait(("edges", k))

        def place(g, carry):
            for h in range(2):
                at = 2 * g + h + off
                s[:, at, LOW - 1, :] = yrecv[k, 0, g, 4 * h : 4 * h + 4, :]
                s[:, at, TOP, :] = yrecv[k, 1, g, 4 * h : 4 * h + 4, :]
            return carry

        lax.fori_loop(0, 8, place, 0)
        column = zrecv[k]

        def plane(x, carry):
            coefs = [coefficients(wc[d, x + 2], fraction) for d in range(3)]
            for f in range(FIELDS):
                ghost = pltpu.roll(column, (127 - 2 * (FIELDS * x + f) + 128) % 128, 1)
                base = tc0[f, x + 3, rows, :]
                new = stepped(s, f, x + off, base, ghost, coefs, fraction, lane)
                if k == 2:
                    sc3[f, x] = new
                else:
                    (uc1, uc2)[k][f, x + 1, rows, :] = new
            return carry

        lax.fori_loop(0, CX, plane, 0)

    fine = [sf0, sf1, sf2]

    def fine_plane(k, x, o, half, first):
        fraction = section_weights[k]
        coefs = [coefficients(wf[d, x + 2], fraction) for d in range(3)]
        column = zface[o, :, 128 * half : 128 * half + 128]
        made = []
        for f in range(FIELDS):
            ghost = pltpu.roll(column, (127 - first - 2 * f + 128) % 128, 1)
            base = sf0[f, x + 3, rows, :]
            new = stepped(fine[k], f, x + 3, base, ghost, coefs, fraction, lane)
            made.append(new)
            if k == 2:
                sf3[f, x] = new
            else:
                fine[k + 1][f, x + 3, rows, :] = new
        return made

    def fine_section(k):
        def pair(j, carry):
            fine_plane(k, 2 * j, 0, 0, 8 * j)
            fine_plane(k, 2 * j + 1, 1, 0, 8 * j)
            return carry

        lax.fori_loop(0, 16, pair, 0)
        fine_plane(k, -1, 1, 1, 0)
        fine_plane(k, FX, 0, 1, 8)
        if k == 0:
            fine_plane(k, -2, 0, 1, 0)
            fine_plane(k, FX + 1, 1, 1, 8)

    per = 16 // CHUNKS

    def last_section():
        def pair(j, carry):
            first = fine_plane(2, 2 * j, 0, 0, 8 * j)
            second = fine_plane(2, 2 * j + 1, 1, 0, 8 * j)
            for f in range(FIELDS):
                pairs[j, f] = first[f] + second[f]
            return carry

        for c in range(CHUNKS):
            lax.fori_loop(c * per, (c + 1) * per, pair, 0)
            blocks = []
            for j in range(c * per, (c + 1) * per):
                for fp in range(2):
                    halves = [
                        pairs[j, 2 * fp + n, pl.ds(0, 8, stride=2), :]
                        + pairs[j, 2 * fp + n, pl.ds(1, 8, stride=2), :]
                        for n in range(2)
                    ]
                    blocks.append(jnp.concatenate(halves, axis=1))
            avgxs[c][0] = split_dot(jnp.concatenate(blocks, axis=0), w_avg[...])
            shift_x(("avg", c), avgxs[c])

    inside = (lane8 >= 32) & (lane8 < 96)

    def merge(c):
        wait((("avg", c), 2))
        result[...] = avgzs[c][1][home[2]].reshape(CHUNK_ROWS // 8, 8, LANES)
        for j in range(per):
            x = c * per + j
            for fp in range(2):
                block = result[2 * j + fp]
                for n in range(2):
                    f = 2 * fp + n
                    moved = pltpu.roll(block, 32 if n == 0 else 96, 1)
                    sc3[f, x, 4:12, :] = jnp.where(inside, moved, sc3[f, x, 4:12, :])

    def pay_z(k, turn):
        source = payxs[k] if turn == 0 else payzs[k][0]
        round_z(("pay", k), turn, source, payzs[k][turn], there)

    def avg_z(c, turn):
        source = avgxs[c] if turn == 0 else avgzs[c][0]
        round_z(("avg", c), turn, source, avgzs[c][turn], home)

    def round_z(name, turn, source, bufs, choice):
        wait((name, turn))
        bufs[1] = source[choice[turn]]
        stride = STRIDES[turn]
        halo[name, turn + 1] = tuple(
            ship(bufs.at[1], bufs.at[slot], along_z(step))
            for slot, step in ((0, stride), (2, -stride))
        )

    pl.semaphore_wait(barrier, len(partners))
    start_halos()
    in_cf.wait()
    send_edges(0)
    in_cw.wait()
    slab_range(0, 1, CX - 1)
    slab_range(1, 2, CX - 2)
    packs = [pack_range(0, 1, 9, pack_start())]
    packs += [pack_range(k, 2, 8, pack_start()) for k in (1, 2)]
    for at in (1, CX + 4):
        tc2[:, at, rows, :] = jnp.zeros((FIELDS, NY, LANES), F32)
    wait("cf")
    packs[0] = pack_range(0, 0, 1, packs[0])
    pack_end(0, pack_range(0, 9, 10, packs[0]))
    shift_x(("pay", 0), payxs[0])
    wait("cw")
    slab_range(0, -2, 1)
    slab_range(0, CX - 1, CX + 2)
    packs[1] = pack_range(1, 0, 2, packs[1])
    pack_end(1, pack_range(1, 8, 10, packs[1]))
    shift_x(("pay", 1), payxs[1])
    slab_range(1, -1, 2)
    slab_range(1, CX - 2, CX + 1)
    packs[2] = pack_range(2, 0, 2, packs[2])
    pack_end(2, pack_range(2, 8, 10, packs[2]))
    shift_x(("pay", 2), payxs[2])
    w_face[...] = refine_weights()
    w_avg[...] = average_weights()
    w_mix[...] = interleave_weights()
    coarse_section(0)
    send_edges(1)
    for k in range(3):
        pay_z(k, 0)
    pay_z(0, 1)
    coarse_section(1)
    send_edges(2)
    for k in (1, 2):
        pay_z(k, 1)
    in_ff.wait()
    in_fw.wait()
    wait("ff", "fw")
    faces(0)
    fine_section(0)
    faces(1)
    fine_section(1)
    faces(2)
    last_section()
    out_fine = load(sf3, fo)
    coarse_section(2)
    for turn in range(2):
        for c in range(CHUNKS):
            avg_z(c, turn)
    for c in range(CHUNKS):
        merge(c)
    out_coarse = load(sc3, co)
    for copy in sent:
        copy.wait_send()
    out_fine.wait()
    out_coarse.wait()


def shards(coarse_fields, coarse_wind, fine_fields, fine_wind, fine_owner):
    anywhere = pl.BlockSpec(memory_space=pltpu.HBM)
    vmem = lambda *shape: pltpu.VMEM(shape, F32)
    scratch = (
        [vmem(FIELDS, CX + 6, 32, LANES)] * 3
        + [vmem(FIELDS, CX + 2, 32, LANES)] * 2
        + [vmem(FIELDS, CX, NY, LANES), vmem(3, CX + 4, NY, LANES)]
        + [vmem(FIELDS, FX + 6, 32, LANES)] * 3
        + [vmem(FIELDS, FX, NY, LANES), vmem(3, FX + 4, NY, LANES)]
        + [
            vmem(3, 2, 8, 8, LANES), vmem(3, 2, 8, 8, LANES),
            vmem(3, NY, LANES), vmem(3, NY, LANES),
            [vmem(RING_X, PAY, LANES)] * 3, [[vmem(3, PAY, LANES)] * 2] * 3,
            vmem(PAY, LANES), vmem(80, LANES), vmem(18, 8, 256),
            vmem(2, 2, NY, LANES), vmem(2, NY, 256),
            vmem(CX, FIELDS, NY, LANES),
            [vmem(RING_X, CHUNK_ROWS, LANES)] * CHUNKS,
            [[vmem(3, CHUNK_ROWS, LANES)] * 2] * CHUNKS,
            vmem(CHUNK_ROWS // 8, 8, LANES),
            pltpu.VMEM((256, 256), BF16), pltpu.VMEM((256, 128), BF16),
            pltpu.VMEM((256, 256), BF16),
            pltpu.SemaphoreType.DMA((COPIES,)), pltpu.SemaphoreType.DMA((COPIES,)),
            pltpu.SemaphoreType.DMA((8,)),
        ]
    )
    return pl.pallas_call(
        kernel,
        out_shape=(
            jax.ShapeDtypeStruct(coarse_fields.shape, F32),
            jax.ShapeDtypeStruct(fine_fields.shape, F32),
        ),
        in_specs=[anywhere] * 4 + [pl.BlockSpec(memory_space=pltpu.SMEM)],
        out_specs=(anywhere, anywhere),
        scratch_shapes=scratch,
        compiler_params=pltpu.CompilerParams(
            collective_id=0, has_side_effects=True, vmem_limit_bytes=63 * 1024 * 1024
        ),
        name="two_level_step",
    )(coarse_fields, coarse_wind, fine_fields, fine_wind, fine_owner.reshape((1,)))


def solution(mesh):
    spec = P(None, "gx", "gy", "gz")
    return jax.shard_map(
        shards,
        mesh=mesh,
        in_specs=(spec, spec, spec, spec, P("gx", "gy", "gz")),
        out_specs=(spec, spec),
        check_vma=False,
    )
```

```python
import functools

import jax
import jax.numpy as jnp
from jax import lax
from jax.experimental import pallas as pl
from jax.experimental.pallas import tpu as pltpu
from jax.sharding import PartitionSpec as P

MESH = pl.DeviceIdType.MESH
F32 = jnp.float32
BF16 = jnp.bfloat16
diffusion = 0.05
section_weights = (1.0 / 3.0, 0.5, 1.0)

RING_X, RING_Z = 4, 8
BOXES = RING_X * RING_Z
FIELDS, CX, FX, NY, LANES = 4, 16, 32, 16, 128
LOW, TOP = 8, 24
PAY = (88, 112, 96)
OUTER = (2, 1, 1)
INNER = ((1, 9), (1, 8), (2, 7))
COLUMNS = (64, 88, 72)
ENDS = (80, 76, 80)
RIM = ((0, 72, 112, 80), (9, 80, 48, 84))
CHUNKS = tuple(tuple(range(4 * c, 4 * c + 4)) for c in range(4))
COPIES = 72
VMEM_LIMIT = 62 * 1024 * 1024
STRIDES = (1, 3)


def split_dot(value, weights):
    high = value.astype(BF16)
    rest = value - high.astype(F32)
    mid = rest.astype(BF16)
    low = (rest - mid.astype(F32)).astype(BF16)
    out = jnp.dot(low, weights, preferred_element_type=F32)
    out = out + jnp.dot(mid, weights, preferred_element_type=F32)
    return out + jnp.dot(high, weights, preferred_element_type=F32)


def refine_weights():
    row = lax.broadcasted_iota(jnp.int32, (256, 256), 0)
    col = lax.broadcasted_iota(jnp.int32, (256, 256), 1)
    side, cell, odd = col // 128, (col % 128) // 2, col % 2
    main = (row < 128) & (row // 64 == side)
    near = main & (row % 64 == cell)
    far = main & (row % 64 == cell + 2 * odd - 1)
    extra = row - 128
    corner = (extra >= 0) & (extra < 4) & (extra // 2 == side)
    corner = corner & (col % 128 == jnp.where(extra % 2 == 0, 0, 127))
    return jnp.where(near, 0.75, jnp.where(far | corner, 0.25, 0.0)).astype(BF16)


def average_weights():
    row = lax.broadcasted_iota(jnp.int32, (256, 128), 0)
    col = lax.broadcasted_iota(jnp.int32, (256, 128), 1)
    hit = (row // 128 == col // 64) & ((row % 128) // 2 == col % 64)
    return jnp.where(hit, 0.125, 0.0).astype(BF16)


def interleave_weights():
    row = lax.broadcasted_iota(jnp.int32, (256, 256), 0)
    col = lax.broadcasted_iota(jnp.int32, (256, 256), 1)
    side, p = row // 128, row % 128
    inner = (p >= 8) & (p < 72) & (col == 2 * (p - 8) + side)
    before = (p >= 4) & (p < 8) & (col == 128 + 2 * (p - 4) + side)
    after = (p >= 72) & (p < 76) & (col == 136 + 2 * (p - 72) + side)
    return jnp.where(inner | before | after, 1.0, 0.0).astype(BF16)


def coefficients(wind, fraction):
    weight = (0.5 * fraction) * wind
    base = diffusion * fraction
    return base - weight, base + weight


def stepped(state, field, at, base, ghost, coefs, fraction, lane):
    q = state[field, at, LOW:TOP, :]
    behind = state[field, at - 1, LOW:TOP, :]
    ahead = state[field, at + 1, LOW:TOP, :]
    below = state[field, at, LOW - 1 : TOP - 1, :]
    above = state[field, at, LOW + 1 : TOP + 1, :]
    low_side = q if ghost is None else jnp.where(lane == 127, ghost, q)
    top_side = q if ghost is None else jnp.where(lane == 0, ghost, q)
    under = pltpu.roll(low_side, 1, 1)
    over = pltpu.roll(top_side, 127, 1)
    (xp, xm), (yp, ym), (zp, zm) = coefs
    total = (xp * ahead + xm * behind) + (yp * above + ym * below) + (zp * over + zm * under)
    return total + (base - (6.0 * diffusion * fraction) * q)


def kernel(
    cf, cw, ff, fw, own, sc3, sf3,
    tc0, tc1, tc2, uc1, uc2, wc, sf0, sf1, sf2, wf,
    ysend, yrecv, zsend, zrecv, payxs, payzs, finals, slab, corner, face, zt, zface,
    pairs, avgxs, avgzs, result, w_face, w_avg, w_mix,
    send_sem, recv_sem, load_sem,
):
    gx, gy, gz = lax.axis_index("gx"), lax.axis_index("gy"), lax.axis_index("gz")
    tz, tx = gx // RING_X, gx % RING_X

    def along_x(step):
        return (tz * RING_X + (tx + step + RING_X) % RING_X, gy, gz)

    def along_z(step):
        return (((tz + step + RING_Z) % RING_Z) * RING_X + tx, gy, gz)

    def along_row(step):
        return ((gx + step + BOXES) % BOXES, gy, gz)

    def along_y(step):
        return (gx, (gy + step + 4) % 4, gz)

    other_z = (gx, gy, 1 - gz)

    sent = []
    halo = {}

    def ship(src, dst, device):
        at = len(sent)
        copy = pltpu.make_async_remote_copy(
            src_ref=src, dst_ref=dst, send_sem=send_sem.at[at], recv_sem=recv_sem.at[at],
            device_id=device, device_id_type=MESH,
        )
        copy.start()
        sent.append(copy)
        return copy

    def wait(*names):
        for name in names:
            for copy in halo.pop(name):
                copy.wait_recv()

    loads = []

    def load(src, dst):
        copy = pltpu.make_async_copy(src, dst, load_sem.at[len(loads)])
        copy.start()
        loads.append(copy)
        return copy

    rows = pl.ds(LOW, NY)
    in_cf = load(cf, tc0.at[:, pl.ds(3, CX), rows, :])
    in_cw = load(cw, wc.at[:, pl.ds(2, CX)])
    in_ff = load(ff, sf0.at[:, pl.ds(3, FX), rows, :])
    in_fw = load(fw, wf.at[:, pl.ds(2, FX)])

    barrier = pltpu.get_barrier_semaphore()
    partners = [along_row(-1), along_row(1), along_y(-1), along_y(1), other_z]
    partners += [along_x(s) for s in (-1, 1, 2)] + [along_z(s) for s in (-3, -1, 1, 3)]
    for partner in partners:
        pl.semaphore_signal(barrier, inc=1, device_id=partner, device_id_type=MESH)

    lane = lax.broadcasted_iota(jnp.int32, (NY, LANES), 1)
    lane8 = lax.broadcasted_iota(jnp.int32, (8, LANES), 1)

    def parts_of(shift):
        part_x = shift % RING_X
        part_z = (shift // RING_X + (tx + part_x) // RING_X) % RING_Z
        signed = part_z - jnp.where(part_z > 4, RING_Z, 0)
        third = (signed + 4) // 3
        return part_x, signed - 3 * third + 4, third

    shift = (own[0] - gx + BOXES) % BOXES
    there = parts_of(shift)
    home = parts_of((BOXES - shift) % BOXES)

    def start_halos(coarse):
        def both(name, src, dst, first, last, width, end, where):
            halo[name] = (
                ship(src.at[:, pl.ds(last, width)], where(dst, 0, width), along_row(1)),
                ship(src.at[:, pl.ds(first, width)], where(dst, end, width), along_row(-1)),
            )

        padded = lambda ref, at, width: ref.at[:, pl.ds(at, width), rows, :]
        plain = lambda ref, at, width: ref.at[:, pl.ds(at, width)]
        if coarse:
            both("cf", cf, tc0, 0, CX - 3, 3, CX + 3, padded)
            both("cw", cw, wc, 0, CX - 2, 2, CX + 2, plain)
        else:
            both("ff", ff, sf0, 0, FX - 3, 3, FX + 3, padded)
            both("fw", fw, wf, 0, FX - 2, 2, FX + 2, plain)

    slabs = [tc0, tc1, tc2]

    def slab_range(k, first, last):
        fraction = section_weights[k]

        def inner(at, carry):
            coefs = [coefficients(wc[d, at - 1], fraction) for d in range(3)]
            for f in range(FIELDS):
                base = tc0[f, at, rows, :]
                new = stepped(slabs[k], f, at, base, None, coefs, fraction, lane)
                slabs[k + 1][f, at, rows, :] = new
            return carry

        lax.fori_loop(first + 3, last + 3, inner, 0)

    def pack_start():
        zero = jnp.zeros((NY, LANES), F32)
        return zero, zero, jnp.zeros((8, LANES), F32)

    def pack_group(k, g, store, lanes_at, ends_at, carry):
        s = slabs[k]
        low_z, high_z, ends = carry
        lows, highs = [], []
        for h in range(2):
            at = 2 * g + h + 3 - OUTER[k]
            lows.append(0.75 * s[:, at, LOW + 3, :] + 0.25 * s[:, at, LOW + 4, :])
            highs.append(0.25 * s[:, at, LOW + 11, :] + 0.75 * s[:, at, LOW + 12, :])
            for f in range(FIELDS):
                p = 8 * g + 4 * h + f + lanes_at
                q = s[f, at, rows, :]
                after = pltpu.roll(q, 127, 1)
                t = jnp.where(lane < 64, 0.75 * q + 0.25 * after, 0.25 * q + 0.75 * after)
                low_z = jnp.where(lane == p, pltpu.roll(t, (p - 31 + 128) % 128, 1), low_z)
                high_z = jnp.where(lane == p, pltpu.roll(t, (p - 95 + 128) % 128, 1), high_z)
        low = jnp.concatenate(lows, axis=0)
        high = jnp.concatenate(highs, axis=0)
        store(jnp.where(lane8 < 64, pltpu.roll(low, 96, 1), pltpu.roll(high, 32, 1)))
        for n, (value, source) in enumerate(((low, 31), (low, 96), (high, 31), (high, 96))):
            to = ends_at + 4 * g + n
            ends = jnp.where(lane8 == to, pltpu.roll(value, (to - source + 128) % 128, 1), ends)
        return low_z, high_z, ends

    def pack_range(k, begin, end, carry):
        def group(g, carry):
            row = pl.multiple_of(8 * g - (8 if k == 0 else 0), 8)

            def store(value):
                payxs[k][0, pl.ds(row, 8), :] = value

            return pack_group(k, g, store, 0, ENDS[k], carry)

        return lax.fori_loop(begin, end, group, carry)

    def pack_rim():
        carry = pack_start()
        for g, row, lanes_at, ends_at in RIM:

            def store(value, row=row):
                payxs[1][0, row : row + 8, :] = value

            carry = pack_group(0, g, store, lanes_at, ends_at - 4 * g, carry)
        return carry

    def pack_end(k, carry, rim=None):
        low_z, high_z, ends = carry
        at = COLUMNS[k]
        more = jnp.zeros((8, LANES), F32)
        if rim is not None:
            low_z, high_z, more = low_z + rim[0], high_z + rim[1], rim[2]
        payxs[k][0, at : at + 8, :] = low_z[3:11, :] + ends
        payxs[k][0, at + 8 : at + 10, :] = low_z[11:13, :]
        payxs[k][0, at + 12 : at + 20, :] = high_z[3:11, :] + more
        payxs[k][0, at + 20 : at + 22, :] = high_z[11:13, :]
        shift_x(("pay", k), payxs[k])

    def shift_x(name, bufs):
        halo[name, 0] = tuple(
            ship(bufs.at[0], bufs.at[slot], along_x(-slot)) for slot in (1, 2, 3)
        )

    def arrive(m):
        wait((("pay", m), 2))
        finals[m][...] = payzs[m][1][there[2]]

    def faces(k, late):
        skip = 8 - 4 * OUTER[k]
        message, first = finals[k], COLUMNS[k]
        cells = message[first : first + 8, :]
        if late:
            other = finals[1][COLUMNS[1] + 12 : COLUMNS[1] + 20, :]
            picks = [(g, finals[1], row, other, at) for g, row, _, at in RIM]
        else:
            begin, end = (1, 9) if k == 0 else (0, 9)
            picks = [
                (g, message, 8 * (g - begin), cells, ENDS[k] + 4 * g) for g in range(begin, end)
            ]
        for g, source, row, ends, ends_at in picks:
            at = 8 * g + skip
            slab[k, at : at + 8, :] = source[row : row + 8, :]
            corner[k, at : at + 8, :] = pltpu.roll(ends, (128 - ends_at) % 128, 1)
        parts = []
        for ref in (slab, corner):
            before, here, after = ref[k, 0:72, :], ref[k, 4:76, :], ref[k, 8:80, :]
            even = 0.25 * before + 0.75 * here
            odd = 0.75 * here + 0.25 * after
            parts.append(jnp.concatenate((even, odd), axis=0))
        made = split_dot(jnp.concatenate(parts, axis=1), w_face[...])
        face[...] = made.reshape(18, 8, 256)
        state = fine[k]

        def place(m, carry):
            for o in range(2):
                block = face[9 * o + m]
                for h in range(2):
                    at = 4 * m + 2 * h + o + 1
                    state[:, at, LOW - 1, :] = block[4 * h : 4 * h + 4, 0:128]
                    state[:, at, TOP, :] = block[4 * h : 4 * h + 4, 128:256]
            return carry

        lax.fori_loop(0, 9, place, 0)

        for side in range(2):
            at = first + 12 * side
            v = message[at : at + 10, :]
            if late:
                at = COLUMNS[1] + 12 * side
                rim = finals[1][at : at + 10, :]
                lane10 = lax.broadcasted_iota(jnp.int32, (10, LANES), 1)
                for g, _, lanes_at, _ in RIM:
                    mine = (lane10 >= 8 * g) & (lane10 < 8 * g + 8)
                    v = jnp.where(mine, pltpu.roll(rim, (128 - lanes_at) % 128, 1), v)
            if skip:
                v = pltpu.roll(v, skip, 1)
            even = 0.25 * pltpu.roll(v, 4, 1) + 0.75 * v
            odd = 0.75 * v + 0.25 * pltpu.roll(v, 124, 1)
            for o, w in enumerate((even, odd)):
                near = 0.75 * w[1:9, :]
                zt[o, side, pl.ds(0, 8, stride=2), :] = 0.25 * w[0:8, :] + near
                zt[o, side, pl.ds(1, 8, stride=2), :] = near + 0.25 * w[2:10, :]
        both = jnp.concatenate(
            [jnp.concatenate((zt[o, 0], zt[o, 1]), axis=1) for o in range(2)], axis=0
        )
        zface[k] = split_dot(both, w_mix[...]).reshape(2, NY, 256)

    def send_edges(k):
        s, off = ((tc0, 3), (uc1, 1), (uc2, 1))[k]
        edge_lane = jnp.where(gz == 0, 127, 0)

        def group(g, acc):
            for h in range(2):
                at = 2 * g + h + off
                ysend[k, 0, g, 4 * h : 4 * h + 4, :] = s[:, at, LOW, :]
                ysend[k, 1, g, 4 * h : 4 * h + 4, :] = s[:, at, TOP - 1, :]
                for f in range(FIELDS):
                    to = 2 * (8 * g + 4 * h + f) + gz
                    moved = pltpu.roll(s[f, at, rows, :], (to - edge_lane + 128) % 128, 1)
                    acc = jnp.where(lane == to, moved, acc)
            return acc

        zsend[k] = lax.fori_loop(0, 8, group, jnp.zeros((NY, LANES), F32))
        copies = [
            ship(ysend.at[k, 1], yrecv.at[k, 0], along_y(1)),
            ship(ysend.at[k, 0], yrecv.at[k, 1], along_y(-1)),
            ship(zsend.at[k], zrecv.at[k], other_z),
        ]
        if k:
            copies += [
                ship(s.at[:, CX, rows, :], s.at[:, 0, rows, :], along_row(1)),
                ship(s.at[:, 1, rows, :], s.at[:, CX + 1, rows, :], along_row(-1)),
            ]
        halo["edges", k] = copies

    def coarse_section(k):
        s, off = ((tc0, 3), (uc1, 1), (uc2, 1))[k]
        fraction = section_weights[k]
        wait(("edges", k))

        def place(g, carry):
            for h in range(2):
                at = 2 * g + h + off
                s[:, at, LOW - 1, :] = yrecv[k, 0, g, 4 * h : 4 * h + 4, :]
                s[:, at, TOP, :] = yrecv[k, 1, g, 4 * h : 4 * h + 4, :]
            return carry

        lax.fori_loop(0, 8, place, 0)
        column = zrecv[k]

        def plane(x, carry):
            coefs = [coefficients(wc[d, x + 2], fraction) for d in range(3)]
            for f in range(FIELDS):
                ghost = pltpu.roll(column, (127 - 2 * (FIELDS * x + f) + 128) % 128, 1)
                base = tc0[f, x + 3, rows, :]
                new = stepped(s, f, x + off, base, ghost, coefs, fraction, lane)
                if k == 2:
                    sc3[f, x] = new
                else:
                    (uc1, uc2)[k][f, x + 1, rows, :] = new
            return carry

        lax.fori_loop(0, CX, plane, 0)

    fine = [sf0, sf1, sf2]

    def fine_plane(k, x, o, half, first):
        fraction = section_weights[k]
        coefs = [coefficients(wf[d, x + 2], fraction) for d in range(3)]
        column = zface[k, o, :, 128 * half : 128 * half + 128]
        made = []
        for f in range(FIELDS):
            ghost = pltpu.roll(column, (127 - first - 2 * f + 128) % 128, 1)
            base = sf0[f, x + 3, rows, :]
            new = stepped(fine[k], f, x + 3, base, ghost, coefs, fraction, lane)
            made.append(new)
            if k == 2:
                sf3[f, x] = new
            else:
                fine[k + 1][f, x + 3, rows, :] = new
        return made

    def pair(k, j):
        return fine_plane(k, 2 * j, 0, 0, 8 * j), fine_plane(k, 2 * j + 1, 1, 0, 8 * j)

    def fine_pairs(k, first, last):
        def step(j, carry):
            pair(k, j)
            return carry

        lax.fori_loop(first, last, step, 0)

    def fine_rim(k):
        fine_plane(k, -1, 1, 1, 0)
        fine_plane(k, FX, 0, 1, 8)
        if k == 0:
            fine_plane(k, -2, 0, 1, 0)
            fine_plane(k, FX + 1, 1, 1, 8)

    def last_section(c):
        js = CHUNKS[c]

        def step(j, carry):
            first, second = pair(2, j)
            for f in range(FIELDS):
                pairs[j, f] = first[f] + second[f]
            return carry

        lax.fori_loop(js[0], js[-1] + 1, step, 0)
        blocks = []
        for j in js:
            for fp in range(2):
                halves = [
                    pairs[j, 2 * fp + n, pl.ds(0, 8, stride=2), :]
                    + pairs[j, 2 * fp + n, pl.ds(1, 8, stride=2), :]
                    for n in range(2)
                ]
                blocks.append(jnp.concatenate(halves, axis=1))
        avgxs[c][0] = split_dot(jnp.concatenate(blocks, axis=0), w_avg[...])
        shift_x(("avg", c), avgxs[c])

    inside = (lane8 >= 32) & (lane8 < 96)

    def merge(c):
        wait((("avg", c), 2))
        js = CHUNKS[c]
        result[0 : 16 * len(js), :] = avgzs[c][1][home[2]]
        for at, x in enumerate(js):
            for fp in range(2):
                block = result[16 * at + 8 * fp : 16 * at + 8 * fp + 8, :]
                for n in range(2):
                    f = 2 * fp + n
                    moved = pltpu.roll(block, 32 if n == 0 else 96, 1)
                    sc3[f, x, 4:12, :] = jnp.where(inside, moved, sc3[f, x, 4:12, :])

    def pay_z(k, turn):
        source = payxs[k] if turn == 0 else payzs[k][0]
        round_z(("pay", k), turn, source, payzs[k][turn], there)

    def avg_z(c, turn):
        source = avgxs[c] if turn == 0 else avgzs[c][0]
        round_z(("avg", c), turn, source, avgzs[c][turn], home)

    def round_z(name, turn, source, bufs, choice):
        wait((name, turn))
        bufs[1] = source[choice[turn]]
        stride = STRIDES[turn]
        halo[name, turn + 1] = tuple(
            ship(bufs.at[1], bufs.at[slot], along_z(step))
            for slot, step in ((0, stride), (2, -stride))
        )

    pl.semaphore_wait(barrier, len(partners))
    start_halos(True)
    in_cf.wait()
    pack_end(0, pack_range(0, *INNER[0], pack_start()))
    in_cw.wait()
    slab_range(0, 1, CX - 1)
    slab_range(1, 2, CX - 2)
    pack1 = pack_range(1, *INNER[1], pack_start())
    pack2 = pack_range(2, *INNER[2], pack_start())
    wait("cf")
    rim = pack_rim()
    wait("cw")
    slab_range(0, -2, 1)
    slab_range(0, CX - 1, CX + 2)
    pack1 = pack_range(1, 0, 1, pack1)
    pack_end(1, pack_range(1, 8, 9, pack1), rim)
    pay_z(0, 0)
    slab_range(1, -1, 2)
    slab_range(1, CX - 2, CX + 1)
    pack2 = pack_range(2, 0, 2, pack2)
    pack_end(2, pack_range(2, 7, 9, pack2))
    send_edges(0)
    pay_z(0, 1)
    w_face[...] = refine_weights()
    w_avg[...] = average_weights()
    w_mix[...] = interleave_weights()
    pay_z(1, 0)
    pay_z(2, 0)
    coarse_section(0)
    send_edges(1)
    pay_z(1, 1)
    pay_z(2, 1)
    start_halos(False)
    in_ff.wait()
    in_fw.wait()
    arrive(0)
    faces(0, False)
    fine_pairs(0, 1, 15)
    arrive(1)
    faces(1, False)
    fine_pairs(1, 2, 14)
    faces(0, True)
    wait("ff", "fw")
    pair(0, jnp.int32(0))
    pair(0, jnp.int32(15))
    fine_rim(0)
    fine_pairs(1, 0, 2)
    fine_pairs(1, 14, 16)
    fine_rim(1)
    arrive(2)
    faces(2, False)
    for c in range(4):
        last_section(c)
    for c in range(4):
        avg_z(c, 0)
    coarse_section(1)
    send_edges(2)
    for c in range(4):
        avg_z(c, 1)
    coarse_section(2)
    for c in range(4):
        merge(c)
    for copy in sent:
        copy.wait_send()


def shards(coarse_fields, coarse_wind, fine_fields, fine_wind, fine_owner):
    anywhere = pl.BlockSpec(memory_space=pltpu.HBM)
    vmem = lambda *shape: pltpu.VMEM(shape, F32)
    scratch = (
        [vmem(FIELDS, CX + 6, 32, LANES)] * 3
        + [vmem(FIELDS, CX + 2, 32, LANES)] * 2
        + [vmem(3, CX + 4, NY, LANES)]
        + [vmem(FIELDS, FX + 6, 32, LANES)] * 3
        + [vmem(3, FX + 4, NY, LANES)]
        + [
            vmem(3, 2, 8, 8, LANES), vmem(3, 2, 8, 8, LANES),
            vmem(3, NY, LANES), vmem(3, NY, LANES),
            [vmem(RING_X, n, LANES) for n in PAY], [[vmem(3, n, LANES)] * 2 for n in PAY],
            [vmem(n, LANES) for n in PAY], vmem(3, 80, LANES), vmem(3, 80, LANES), vmem(18, 8, 256),
            vmem(2, 2, NY, LANES), vmem(3, 2, NY, 256),
            vmem(CX, FIELDS, NY, LANES),
            [vmem(RING_X, 16 * len(js), LANES) for js in CHUNKS],
            [[vmem(3, 16 * len(js), LANES)] * 2 for js in CHUNKS],
            vmem(16 * len(CHUNKS[0]), LANES),
            pltpu.VMEM((256, 256), BF16), pltpu.VMEM((256, 128), BF16),
            pltpu.VMEM((256, 256), BF16),
            pltpu.SemaphoreType.DMA((COPIES,)), pltpu.SemaphoreType.DMA((COPIES,)),
            pltpu.SemaphoreType.DMA((8,)),
        ]
    )
    results = pl.pallas_call(
        kernel,
        out_shape=(
            pltpu.VMEM(coarse_fields.shape, F32),
            pltpu.VMEM(fine_fields.shape, F32),
        ),
        in_specs=[anywhere] * 4 + [pl.BlockSpec(memory_space=pltpu.SMEM)],
        out_specs=(pl.BlockSpec(memory_space=pltpu.VMEM),) * 2,
        scratch_shapes=scratch,
        compiler_params=pltpu.CompilerParams(
            collective_id=0, has_side_effects=True, vmem_limit_bytes=VMEM_LIMIT
        ),
        name="two_level_step",
    )(coarse_fields, coarse_wind, fine_fields, fine_wind, fine_owner.reshape((1,)))
    return pl.pallas_call(
        write_out,
        out_shape=(
            jax.ShapeDtypeStruct(coarse_fields.shape, F32),
            jax.ShapeDtypeStruct(fine_fields.shape, F32),
        ),
        in_specs=[pl.BlockSpec(memory_space=pl.ANY)] * 2,
        out_specs=(anywhere, anywhere),
        scratch_shapes=[pltpu.SemaphoreType.DMA((2,))],
        compiler_params=pltpu.CompilerParams(vmem_limit_bytes=1024 * 1024),
        name="write_out",
    )(*results)


def write_out(coarse, fine, coarse_out, fine_out, sem):
    first = pltpu.make_async_copy(fine, fine_out, sem.at[0])
    second = pltpu.make_async_copy(coarse, coarse_out, sem.at[1])
    first.start()
    second.start()
    first.wait()
    second.wait()


def solution(mesh):
    spec = P(None, "gx", "gy", "gz")
    return jax.shard_map(
        shards,
        mesh=mesh,
        in_specs=(spec, spec, spec, spec, P("gx", "gy", "gz")),
        out_specs=(spec, spec),
        check_vma=False,
    )
```

```python
import functools

import jax
import jax.numpy as jnp
from jax import lax
from jax.experimental import pallas as pl
from jax.experimental.pallas import tpu as pltpu
from jax.sharding import PartitionSpec as P

MESH = pl.DeviceIdType.MESH
F32 = jnp.float32
BF16 = jnp.bfloat16
diffusion = 0.05
section_weights = (1.0 / 3.0, 0.5, 1.0)

RING_X, RING_Z = 4, 8
BOXES = RING_X * RING_Z
FIELDS, CX, FX, NY, LANES = 4, 16, 32, 16, 128
LOW, TOP = 8, 24
PAY = (88, 112, 96)
OUTER = (2, 1, 1)
INNER = ((1, 9), (1, 8), (2, 7))
COLUMNS = (64, 88, 72)
ENDS = (80, 76, 80)
RIM = ((0, 72, 112, 80), (9, 80, 48, 84))
CHUNKS = tuple(tuple(range(4 * c, 4 * c + 4)) for c in range(4))
COPIES = 72
VMEM_LIMIT = 62 * 1024 * 1024
STRIDES = (1, 3)


def split_dot(value, weights):
    high = value.astype(BF16)
    rest = value - high.astype(F32)
    mid = rest.astype(BF16)
    low = (rest - mid.astype(F32)).astype(BF16)
    out = jnp.dot(low, weights, preferred_element_type=F32)
    out = out + jnp.dot(mid, weights, preferred_element_type=F32)
    return out + jnp.dot(high, weights, preferred_element_type=F32)


def refine_weights():
    row = lax.broadcasted_iota(jnp.int32, (256, 256), 0)
    col = lax.broadcasted_iota(jnp.int32, (256, 256), 1)
    side, cell, odd = col // 128, (col % 128) // 2, col % 2
    main = (row < 128) & (row // 64 == side)
    near = main & (row % 64 == cell)
    far = main & (row % 64 == cell + 2 * odd - 1)
    extra = row - 128
    corner = (extra >= 0) & (extra < 4) & (extra // 2 == side)
    corner = corner & (col % 128 == jnp.where(extra % 2 == 0, 0, 127))
    return jnp.where(near, 0.75, jnp.where(far | corner, 0.25, 0.0)).astype(BF16)


def average_weights():
    row = lax.broadcasted_iota(jnp.int32, (256, 128), 0)
    col = lax.broadcasted_iota(jnp.int32, (256, 128), 1)
    hit = (row // 128 == col // 64) & ((row % 128) // 2 == col % 64)
    return jnp.where(hit, 0.125, 0.0).astype(BF16)


def interleave_weights():
    row = lax.broadcasted_iota(jnp.int32, (256, 256), 0)
    col = lax.broadcasted_iota(jnp.int32, (256, 256), 1)
    side, p = row // 128, row % 128
    inner = (p >= 8) & (p < 72) & (col == 2 * (p - 8) + side)
    before = (p >= 4) & (p < 8) & (col == 128 + 2 * (p - 4) + side)
    after = (p >= 72) & (p < 76) & (col == 136 + 2 * (p - 72) + side)
    return jnp.where(inner | before | after, 1.0, 0.0).astype(BF16)


def coefficients(wind, fraction):
    weight = (0.5 * fraction) * wind
    base = diffusion * fraction
    return base - weight, base + weight


def stepped(state, field, at, base, ghost, coefs, fraction, lane):
    q = state[field, at, LOW:TOP, :]
    behind = state[field, at - 1, LOW:TOP, :]
    ahead = state[field, at + 1, LOW:TOP, :]
    below = state[field, at, LOW - 1 : TOP - 1, :]
    above = state[field, at, LOW + 1 : TOP + 1, :]
    low_side = q if ghost is None else jnp.where(lane == 127, ghost, q)
    top_side = q if ghost is None else jnp.where(lane == 0, ghost, q)
    under = pltpu.roll(low_side, 1, 1)
    over = pltpu.roll(top_side, 127, 1)
    (xp, xm), (yp, ym), (zp, zm) = coefs
    total = (xp * ahead + xm * behind) + (yp * above + ym * below) + (zp * over + zm * under)
    return total + (base - (6.0 * diffusion * fraction) * q)


def kernel(
    cf, cw, ff, fw, own, sc3, sf3,
    tc0, tc1, tc2, uc1, uc2, wc, sf0, sf1, sf2, wf,
    ysend, yrecv, zsend, zrecv, payxs, payzs, finals, slab, corner, face, zt, zface,
    pairs, avgxs, avgzs, result, w_face, w_avg, w_mix,
    send_sem, recv_sem, load_sem,
):
    gx, gy, gz = lax.axis_index("gx"), lax.axis_index("gy"), lax.axis_index("gz")
    tz, tx = gx // RING_X, gx % RING_X

    def along_x(step):
        return (tz * RING_X + (tx + step + RING_X) % RING_X, gy, gz)

    def along_z(step):
        return (((tz + step + RING_Z) % RING_Z) * RING_X + tx, gy, gz)

    def along_row(step):
        return ((gx + step + BOXES) % BOXES, gy, gz)

    def along_y(step):
        return (gx, (gy + step + 4) % 4, gz)

    other_z = (gx, gy, 1 - gz)

    sent = []
    halo = {}

    def ship(src, dst, device):
        at = len(sent)
        copy = pltpu.make_async_remote_copy(
            src_ref=src, dst_ref=dst, send_sem=send_sem.at[at], recv_sem=recv_sem.at[at],
            device_id=device, device_id_type=MESH,
        )
        copy.start()
        sent.append(copy)
        return copy

    def wait(*names):
        for name in names:
            for copy in halo.pop(name):
                copy.wait_recv()

    loads = []

    def load(src, dst):
        copy = pltpu.make_async_copy(src, dst, load_sem.at[len(loads)])
        copy.start()
        loads.append(copy)
        return copy

    rows = pl.ds(LOW, NY)
    in_cf = load(cf, tc0.at[:, pl.ds(3, CX), rows, :])
    in_cw = load(cw, wc.at[:, pl.ds(2, CX)])
    in_ff = load(ff, sf0.at[:, pl.ds(3, FX), rows, :])
    in_fw = load(fw, wf.at[:, pl.ds(2, FX)])

    barrier = pltpu.get_barrier_semaphore()
    partners = [along_row(-1), along_row(1), along_y(-1), along_y(1), other_z]
    partners += [along_x(s) for s in (-1, 1, 2)] + [along_z(s) for s in (-3, -1, 1, 3)]
    for partner in partners:
        pl.semaphore_signal(barrier, inc=1, device_id=partner, device_id_type=MESH)

    lane = lax.broadcasted_iota(jnp.int32, (NY, LANES), 1)
    lane8 = lax.broadcasted_iota(jnp.int32, (8, LANES), 1)

    def parts_of(shift):
        part_x = shift % RING_X
        part_z = (shift // RING_X + (tx + part_x) // RING_X) % RING_Z
        signed = part_z - jnp.where(part_z > 4, RING_Z, 0)
        third = (signed + 4) // 3
        return part_x, signed - 3 * third + 4, third

    shift = (own[0] - gx + BOXES) % BOXES
    there = parts_of(shift)
    home = parts_of((BOXES - shift) % BOXES)

    def start_halos(coarse):
        def both(name, src, dst, first, last, width, end, where):
            halo[name] = (
                ship(src.at[:, pl.ds(last, width)], where(dst, 0, width), along_row(1)),
                ship(src.at[:, pl.ds(first, width)], where(dst, end, width), along_row(-1)),
            )

        padded = lambda ref, at, width: ref.at[:, pl.ds(at, width), rows, :]
        plain = lambda ref, at, width: ref.at[:, pl.ds(at, width)]
        if coarse:
            both("cf", cf, tc0, 0, CX - 3, 3, CX + 3, padded)
            both("cw", cw, wc, 0, CX - 2, 2, CX + 2, plain)
        else:
            both("ff", ff, sf0, 0, FX - 3, 3, FX + 3, padded)
            both("fw", fw, wf, 0, FX - 2, 2, FX + 2, plain)

    slabs = [tc0, tc1, tc2]

    def slab_range(k, first, last):
        fraction = section_weights[k]

        def inner(at, carry):
            coefs = [coefficients(wc[d, at - 1], fraction) for d in range(3)]
            for f in range(FIELDS):
                base = tc0[f, at, rows, :]
                new = stepped(slabs[k], f, at, base, None, coefs, fraction, lane)
                slabs[k + 1][f, at, rows, :] = new
            return carry

        lax.fori_loop(first + 3, last + 3, inner, 0)

    def pack_start():
        zero = jnp.zeros((NY, LANES), F32)
        return zero, zero, jnp.zeros((8, LANES), F32)

    def pack_group(k, g, store, lanes_at, ends_at, carry):
        s = slabs[k]
        low_z, high_z, ends = carry
        lows, highs = [], []
        for h in range(2):
            at = 2 * g + h + 3 - OUTER[k]
            lows.append(0.75 * s[:, at, LOW + 3, :] + 0.25 * s[:, at, LOW + 4, :])
            highs.append(0.25 * s[:, at, LOW + 11, :] + 0.75 * s[:, at, LOW + 12, :])
            for f in range(FIELDS):
                p = 8 * g + 4 * h + f + lanes_at
                q = s[f, at, rows, :]
                after = pltpu.roll(q, 127, 1)
                t = jnp.where(lane < 64, 0.75 * q + 0.25 * after, 0.25 * q + 0.75 * after)
                low_z = jnp.where(lane == p, pltpu.roll(t, (p - 31 + 128) % 128, 1), low_z)
                high_z = jnp.where(lane == p, pltpu.roll(t, (p - 95 + 128) % 128, 1), high_z)
        low = jnp.concatenate(lows, axis=0)
        high = jnp.concatenate(highs, axis=0)
        store(jnp.where(lane8 < 64, pltpu.roll(low, 96, 1), pltpu.roll(high, 32, 1)))
        for n, (value, source) in enumerate(((low, 31), (low, 96), (high, 31), (high, 96))):
            to = ends_at + 4 * g + n
            ends = jnp.where(lane8 == to, pltpu.roll(value, (to - source + 128) % 128, 1), ends)
        return low_z, high_z, ends

    def pack_range(k, begin, end, carry):
        def group(g, carry):
            row = pl.multiple_of(8 * g - (8 if k == 0 else 0), 8)

            def store(value):
                payxs[k][0, pl.ds(row, 8), :] = value

            return pack_group(k, g, store, 0, ENDS[k], carry)

        return lax.fori_loop(begin, end, group, carry)

    def pack_rim():
        carry = pack_start()
        for g, row, lanes_at, ends_at in RIM:

            def store(value, row=row):
                payxs[1][0, row : row + 8, :] = value

            carry = pack_group(0, g, store, lanes_at, ends_at - 4 * g, carry)
        return carry

    def pack_end(k, carry, rim=None):
        low_z, high_z, ends = carry
        at = COLUMNS[k]
        more = jnp.zeros((8, LANES), F32)
        if rim is not None:
            low_z, high_z, more = low_z + rim[0], high_z + rim[1], rim[2]
        payxs[k][0, at : at + 8, :] = low_z[3:11, :] + ends
        payxs[k][0, at + 8 : at + 10, :] = low_z[11:13, :]
        payxs[k][0, at + 12 : at + 20, :] = high_z[3:11, :] + more
        payxs[k][0, at + 20 : at + 22, :] = high_z[11:13, :]
        shift_x(("pay", k), payxs[k])

    def shift_x(name, bufs):
        halo[name, 0] = tuple(
            ship(bufs.at[0], bufs.at[slot], along_x(-slot)) for slot in (1, 2, 3)
        )

    def arrive(m):
        wait((("pay", m), 2))
        finals[m][...] = payzs[m][1][there[2]]

    def faces(k, late):
        skip = 8 - 4 * OUTER[k]
        message, first = finals[k], COLUMNS[k]
        cells = message[first : first + 8, :]
        if late:
            other = finals[1][COLUMNS[1] + 12 : COLUMNS[1] + 20, :]
            picks = [(g, finals[1], row, other, at) for g, row, _, at in RIM]
        else:
            begin, end = (1, 9) if k == 0 else (0, 9)
            picks = [
                (g, message, 8 * (g - begin), cells, ENDS[k] + 4 * g) for g in range(begin, end)
            ]
        for g, source, row, ends, ends_at in picks:
            at = 8 * g + skip
            slab[k, at : at + 8, :] = source[row : row + 8, :]
            corner[k, at : at + 8, :] = pltpu.roll(ends, (128 - ends_at) % 128, 1)
        parts = []
        for ref in (slab, corner):
            before, here, after = ref[k, 0:72, :], ref[k, 4:76, :], ref[k, 8:80, :]
            even = 0.25 * before + 0.75 * here
            odd = 0.75 * here + 0.25 * after
            parts.append(jnp.concatenate((even, odd), axis=0))
        made = split_dot(jnp.concatenate(parts, axis=1), w_face[...])
        face[...] = made.reshape(18, 8, 256)
        state = fine[k]

        def place(m, carry):
            for o in range(2):
                block = face[9 * o + m]
                for h in range(2):
                    at = 4 * m + 2 * h + o + 1
                    state[:, at, LOW - 1, :] = block[4 * h : 4 * h + 4, 0:128]
                    state[:, at, TOP, :] = block[4 * h : 4 * h + 4, 128:256]
            return carry

        lax.fori_loop(0, 9, place, 0)

        for side in range(2):
            at = first + 12 * side
            v = message[at : at + 10, :]
            if late:
                at = COLUMNS[1] + 12 * side
                rim = finals[1][at : at + 10, :]
                lane10 = lax.broadcasted_iota(jnp.int32, (10, LANES), 1)
                for g, _, lanes_at, _ in RIM:
                    mine = (lane10 >= 8 * g) & (lane10 < 8 * g + 8)
                    v = jnp.where(mine, pltpu.roll(rim, (128 - lanes_at) % 128, 1), v)
            if skip:
                v = pltpu.roll(v, skip, 1)
            even = 0.25 * pltpu.roll(v, 4, 1) + 0.75 * v
            odd = 0.75 * v + 0.25 * pltpu.roll(v, 124, 1)
            for o, w in enumerate((even, odd)):
                near = 0.75 * w[1:9, :]
                zt[o, side, pl.ds(0, 8, stride=2), :] = 0.25 * w[0:8, :] + near
                zt[o, side, pl.ds(1, 8, stride=2), :] = near + 0.25 * w[2:10, :]
        both = jnp.concatenate(
            [jnp.concatenate((zt[o, 0], zt[o, 1]), axis=1) for o in range(2)], axis=0
        )
        zface[k] = split_dot(both, w_mix[...]).reshape(2, NY, 256)

    def send_edges(k):
        s, off = ((tc0, 3), (uc1, 1), (uc2, 1))[k]
        edge_lane = jnp.where(gz == 0, 127, 0)

        def group(g, acc):
            for h in range(2):
                at = 2 * g + h + off
                ysend[k, 0, g, 4 * h : 4 * h + 4, :] = s[:, at, LOW, :]
                ysend[k, 1, g, 4 * h : 4 * h + 4, :] = s[:, at, TOP - 1, :]
                for f in range(FIELDS):
                    to = 2 * (8 * g + 4 * h + f) + gz
                    moved = pltpu.roll(s[f, at, rows, :], (to - edge_lane + 128) % 128, 1)
                    acc = jnp.where(lane == to, moved, acc)
            return acc

        zsend[k] = lax.fori_loop(0, 8, group, jnp.zeros((NY, LANES), F32))
        copies = [
            ship(ysend.at[k, 1], yrecv.at[k, 0], along_y(1)),
            ship(ysend.at[k, 0], yrecv.at[k, 1], along_y(-1)),
            ship(zsend.at[k], zrecv.at[k], other_z),
        ]
        if k:
            copies += [
                ship(s.at[:, CX, rows, :], s.at[:, 0, rows, :], along_row(1)),
                ship(s.at[:, 1, rows, :], s.at[:, CX + 1, rows, :], along_row(-1)),
            ]
        halo["edges", k] = copies

    def coarse_section(k):
        s, off = ((tc0, 3), (uc1, 1), (uc2, 1))[k]
        fraction = section_weights[k]
        wait(("edges", k))

        def place(g, carry):
            for h in range(2):
                at = 2 * g + h + off
                s[:, at, LOW - 1, :] = yrecv[k, 0, g, 4 * h : 4 * h + 4, :]
                s[:, at, TOP, :] = yrecv[k, 1, g, 4 * h : 4 * h + 4, :]
            return carry

        lax.fori_loop(0, 8, place, 0)
        column = zrecv[k]

        def plane(x, carry):
            coefs = [coefficients(wc[d, x + 2], fraction) for d in range(3)]
            for f in range(FIELDS):
                ghost = pltpu.roll(column, (127 - 2 * (FIELDS * x + f) + 128) % 128, 1)
                base = tc0[f, x + 3, rows, :]
                new = stepped(s, f, x + off, base, ghost, coefs, fraction, lane)
                if k == 2:
                    sc3[f, x] = new
                else:
                    (uc1, uc2)[k][f, x + 1, rows, :] = new
            return carry

        lax.fori_loop(0, CX, plane, 0)

    fine = [sf0, sf1, sf2]

    def fine_plane(k, x, o, half, first):
        fraction = section_weights[k]
        coefs = [coefficients(wf[d, x + 2], fraction) for d in range(3)]
        column = zface[k, o, :, 128 * half : 128 * half + 128]
        made = []
        for f in range(FIELDS):
            ghost = pltpu.roll(column, (127 - first - 2 * f + 128) % 128, 1)
            base = sf0[f, x + 3, rows, :]
            new = stepped(fine[k], f, x + 3, base, ghost, coefs, fraction, lane)
            made.append(new)
            if k == 2:
                sf3[f, x] = new
            else:
                fine[k + 1][f, x + 3, rows, :] = new
        return made

    def pair(k, j):
        return fine_plane(k, 2 * j, 0, 0, 8 * j), fine_plane(k, 2 * j + 1, 1, 0, 8 * j)

    def fine_pairs(k, first, last):
        def step(j, carry):
            pair(k, j)
            return carry

        lax.fori_loop(first, last, step, 0)

    def fine_rim(k):
        fine_plane(k, -1, 1, 1, 0)
        fine_plane(k, FX, 0, 1, 8)
        if k == 0:
            fine_plane(k, -2, 0, 1, 0)
            fine_plane(k, FX + 1, 1, 1, 8)

    def last_section(c):
        js = CHUNKS[c]

        def step(j, carry):
            first, second = pair(2, j)
            for f in range(FIELDS):
                pairs[j, f] = first[f] + second[f]
            return carry

        lax.fori_loop(js[0], js[-1] + 1, step, 0)
        blocks = []
        for j in js:
            for fp in range(2):
                halves = [
                    pairs[j, 2 * fp + n, pl.ds(0, 8, stride=2), :]
                    + pairs[j, 2 * fp + n, pl.ds(1, 8, stride=2), :]
                    for n in range(2)
                ]
                blocks.append(jnp.concatenate(halves, axis=1))
        avgxs[c][0] = split_dot(jnp.concatenate(blocks, axis=0), w_avg[...])
        shift_x(("avg", c), avgxs[c])

    inside = (lane8 >= 32) & (lane8 < 96)

    def merge(c):
        wait((("avg", c), 2))
        js = CHUNKS[c]
        result[0 : 16 * len(js), :] = avgzs[c][1][home[2]]
        for at, x in enumerate(js):
            for fp in range(2):
                block = result[16 * at + 8 * fp : 16 * at + 8 * fp + 8, :]
                for n in range(2):
                    f = 2 * fp + n
                    moved = pltpu.roll(block, 32 if n == 0 else 96, 1)
                    sc3[f, x, 4:12, :] = jnp.where(inside, moved, sc3[f, x, 4:12, :])

    def pay_z(k, turn):
        source = payxs[k] if turn == 0 else payzs[k][0]
        round_z(("pay", k), turn, source, payzs[k][turn], there)

    def avg_z(c, turn):
        source = avgxs[c] if turn == 0 else avgzs[c][0]
        round_z(("avg", c), turn, source, avgzs[c][turn], home)

    def round_z(name, turn, source, bufs, choice):
        wait((name, turn))
        bufs[1] = source[choice[turn]]
        stride = STRIDES[turn]
        halo[name, turn + 1] = tuple(
            ship(bufs.at[1], bufs.at[slot], along_z(step))
            for slot, step in ((0, stride), (2, -stride))
        )

    pl.semaphore_wait(barrier, len(partners))
    start_halos(True)
    in_cf.wait()
    pack_end(0, pack_range(0, *INNER[0], pack_start()))
    in_cw.wait()
    slab_range(0, 1, CX - 1)
    slab_range(1, 2, CX - 2)
    pack1 = pack_range(1, *INNER[1], pack_start())
    pack2 = pack_range(2, *INNER[2], pack_start())
    wait("cf")
    rim = pack_rim()
    wait("cw")
    slab_range(0, -2, 1)
    slab_range(0, CX - 1, CX + 2)
    pack1 = pack_range(1, 0, 1, pack1)
    pack_end(1, pack_range(1, 8, 9, pack1), rim)
    pay_z(0, 0)
    slab_range(1, -1, 2)
    slab_range(1, CX - 2, CX + 1)
    pack2 = pack_range(2, 0, 2, pack2)
    pack_end(2, pack_range(2, 7, 9, pack2))
    send_edges(0)
    pay_z(0, 1)
    w_face[...] = refine_weights()
    w_avg[...] = average_weights()
    w_mix[...] = interleave_weights()
    pay_z(1, 0)
    pay_z(2, 0)
    start_halos(False)
    coarse_section(0)
    send_edges(1)
    pay_z(1, 1)
    pay_z(2, 1)
    in_ff.wait()
    in_fw.wait()
    arrive(0)
    faces(0, False)
    fine_pairs(0, 1, 15)
    arrive(1)
    faces(1, False)
    fine_pairs(1, 2, 14)
    faces(0, True)
    wait("ff", "fw")
    pair(0, jnp.int32(0))
    pair(0, jnp.int32(15))
    fine_rim(0)
    fine_pairs(1, 0, 2)
    fine_pairs(1, 14, 16)
    fine_rim(1)
    arrive(2)
    faces(2, False)
    for c in range(4):
        last_section(c)
    for c in range(4):
        avg_z(c, 0)
    coarse_section(1)
    send_edges(2)
    for c in range(4):
        avg_z(c, 1)
    coarse_section(2)
    for c in range(4):
        merge(c)
    for copy in sent:
        copy.wait_send()


def shards(coarse_fields, coarse_wind, fine_fields, fine_wind, fine_owner):
    anywhere = pl.BlockSpec(memory_space=pltpu.HBM)
    vmem = lambda *shape: pltpu.VMEM(shape, F32)
    scratch = (
        [vmem(FIELDS, CX + 6, 32, LANES)] * 3
        + [vmem(FIELDS, CX + 2, 32, LANES)] * 2
        + [vmem(3, CX + 4, NY, LANES)]
        + [vmem(FIELDS, FX + 6, 32, LANES)] * 3
        + [vmem(3, FX + 4, NY, LANES)]
        + [
            vmem(3, 2, 8, 8, LANES), vmem(3, 2, 8, 8, LANES),
            vmem(3, NY, LANES), vmem(3, NY, LANES),
            [vmem(RING_X, n, LANES) for n in PAY], [[vmem(3, n, LANES)] * 2 for n in PAY],
            [vmem(n, LANES) for n in PAY], vmem(3, 80, LANES), vmem(3, 80, LANES), vmem(18, 8, 256),
            vmem(2, 2, NY, LANES), vmem(3, 2, NY, 256),
            vmem(CX, FIELDS, NY, LANES),
            [vmem(RING_X, 16 * len(js), LANES) for js in CHUNKS],
            [[vmem(3, 16 * len(js), LANES)] * 2 for js in CHUNKS],
            vmem(16 * len(CHUNKS[0]), LANES),
            pltpu.VMEM((256, 256), BF16), pltpu.VMEM((256, 128), BF16),
            pltpu.VMEM((256, 256), BF16),
            pltpu.SemaphoreType.DMA((COPIES,)), pltpu.SemaphoreType.DMA((COPIES,)),
            pltpu.SemaphoreType.DMA((8,)),
        ]
    )
    results = pl.pallas_call(
        kernel,
        out_shape=(
            pltpu.VMEM(coarse_fields.shape, F32),
            pltpu.VMEM(fine_fields.shape, F32),
        ),
        in_specs=[anywhere] * 4 + [pl.BlockSpec(memory_space=pltpu.SMEM)],
        out_specs=(pl.BlockSpec(memory_space=pltpu.VMEM),) * 2,
        scratch_shapes=scratch,
        compiler_params=pltpu.CompilerParams(
            collective_id=0, has_side_effects=True, vmem_limit_bytes=VMEM_LIMIT
        ),
        name="two_level_step",
    )(coarse_fields, coarse_wind, fine_fields, fine_wind, fine_owner.reshape((1,)))
    return pl.pallas_call(
        write_out,
        out_shape=(
            jax.ShapeDtypeStruct(coarse_fields.shape, F32),
            jax.ShapeDtypeStruct(fine_fields.shape, F32),
        ),
        in_specs=[pl.BlockSpec(memory_space=pl.ANY)] * 2,
        out_specs=(anywhere, anywhere),
        scratch_shapes=[pltpu.SemaphoreType.DMA((2,))],
        compiler_params=pltpu.CompilerParams(vmem_limit_bytes=1024 * 1024),
        name="write_out",
    )(*results)


def write_out(coarse, fine, coarse_out, fine_out, sem):
    first = pltpu.make_async_copy(fine, fine_out, sem.at[0])
    second = pltpu.make_async_copy(coarse, coarse_out, sem.at[1])
    first.start()
    second.start()
    first.wait()
    second.wait()


def solution(mesh):
    spec = P(None, "gx", "gy", "gz")
    return jax.shard_map(
        shards,
        mesh=mesh,
        in_specs=(spec, spec, spec, spec, P("gx", "gy", "gz")),
        out_specs=(spec, spec),
        check_vma=False,
    )
```
